32 devices in a mesh: dp: 2 (over core), row: 4 (over y, x), col: 4 (over z).
Axes of the slice: x: 2, y: 2, z: 4, core: 2. Of those that a mesh axis runs over, the one named last changes fastest.
Arguments:
- inputs: bfloat16 [2, 16, 4, 16, 2048], P('dp', 'row', None, None, 'col'), may hold values from -6 to 6
- up_weight: bfloat16 [2048, 4096], P(None, 'col'), may hold values from -0.1875 to 0.1875
- down_weight: bfloat16 [2048, 4096], P(None, 'col'), may hold values from -0.125 to 0.125
- kernel: float32 [125, 4096], P(None, 'col'), may hold values from -0.625 to 0.625
- cotangent: bfloat16 [2, 16, 4, 16, 2048], P('dp', 'row', None, None, 'col'), may hold values from -2 to 2
Outputs:
- block_output: bfloat16 [2, 16, 4, 16, 2048], P('dp', 'row', None, None, 'col')
- input_grad: bfloat16 [2, 16, 4, 16, 2048], P('dp', 'row', None, None, 'col')
- up_grad: bfloat16 [2048, 4096], P(('dp', 'row'), 'col')
- down_grad: bfloat16 [2048, 4096], P(('dp', 'row'), 'col')
- kernel_grad: float32 [125, 4096], P(None, 'col')
The draws below stay inside these ranges and needn't reach their ends.
All inputs are finite; a program needn't handle non-finite values.
Results may differ from the reference program's by a relative error of at most 0.012.
Values may be sent and summed in bfloat16 or wider, within the bound.
A program may use at most 128 MiB of HBM per device.

```python
import jax
import jax.numpy as jnp
from jax import lax

WIDTH = 2048
EXPAND = 4096
TAPS = 125
STATES_DEV = 1
PLANES = 4
TILE_X = 4
TILE_Y = 16
STATES = 2
DEPTH = 16
N_DP = 2
N_ROW = 4
N_COL = 4


def strengthened(entries, key, source, target, shards_of, factor):
    def block_of(axis_at):
        return (jnp.arange(entries.shape[axis_at]) // (entries.shape[axis_at] // shards_of)).reshape((-1,) + (1,) * (entries.ndim - 1 - axis_at))

    one_side = jax.random.permutation(key, shards_of)[block_of(target)]
    other_side = (block_of(target) + shards_of // 2) % shards_of
    return jnp.where((block_of(source) == one_side) | (block_of(source) == other_side), factor * entries, entries)


def levels(rng, dims, shards, low, largest):
    def one(dim, shards_of):
        heights = jax.random.uniform(jax.random.fold_in(jax.random.fold_in(rng, 6), dim), (shards_of,), jnp.float32, low / len(shards), largest / len(shards))
        return jnp.repeat(jnp.exp(heights), dims[dim] // shards_of).reshape((-1,) + (1,) * (len(dims) - dim - 1))

    level = one(*shards[0])
    for cut in shards[1:]:
        level = level * one(*cut)
    return level


def scatter_about(key, dims, width, bound, cuts=(), kind=jnp.bfloat16):
    array = jax.random.normal(key, dims, jnp.float32) * width
    if len(cuts) > 0:
        array = levels(key, dims, cuts, -0.22, 0.18) * array
    return jnp.clip(array, min=-bound, max=bound).astype(kind)


def gaussian_with(own_key, dims, scale, bound, cuts, heavy, held_as=jnp.bfloat16):
    array = scale * jax.random.normal(own_key, dims, jnp.float32)
    if cuts:
        array = array * levels(own_key, dims, cuts, -0.22, 0.18)
    return jnp.clip(strengthened(array, jax.random.fold_in(own_key, 3), *heavy), -bound, bound).astype(held_as)


def setup_inputs(seed: int = 0) -> dict:
    keys = jax.random.split(jax.random.key(seed), 6)
    return {
        "inputs": scatter_about(keys[0], (STATES, DEPTH, TILE_X, TILE_Y, WIDTH), 1.0, 6.0, ((0, 2), (1, 4), (4, 4))),
        "up_weight": gaussian_with(keys[1], (WIDTH, EXPAND), WIDTH ** -0.5, 0.1875, ((1, 4),), (1, 0, 4, 2.0)),
        "down_weight": gaussian_with(keys[2], (WIDTH, EXPAND), EXPAND ** -0.5, 0.125, ((1, 4),), (1, 0, 4, 2.0)),
        "kernel": scatter_about(keys[3], (TAPS, EXPAND), 0.1, 0.625, ((1, 4),), jnp.float32),
        "cotangent": gaussian_with(keys[4], (STATES, DEPTH, TILE_X, TILE_Y, WIDTH), 0.25, 2.0, ((0, 2), (1, 4), (4, 4)), (1, 4, 4, 2.0)),
    }


def pad_field(field):
    return jnp.pad(field, ((0, 0), (2, 2), (2, 2), (2, 2), (0, 0)))


def stencil_sum(padded, kernel, mirror, planes, tile_x, tile_y):
    result = jnp.zeros(padded.shape[:1] + (planes, tile_x, tile_y, padded.shape[4]), jnp.float32)
    for depth_step in range(5):
        for row_step in range(5):
            for col_step in range(5):
                first_z = depth_step + mirror * (4 - 2 * depth_step)
                first_x = row_step + mirror * (4 - 2 * row_step)
                first_y = col_step + mirror * (4 - 2 * col_step)
                window = padded[:, first_z:first_z + planes, first_x:first_x + tile_x, first_y:first_y + tile_y, :]
                result = result + kernel[25 * depth_step + 5 * row_step + col_step] * window
    return result


def kernel_terms(padded, grad_field, planes, tile_x, tile_y):
    grad_wide = grad_field.astype(jnp.float32)
    rows_list = []
    for depth_step in range(5):
        for row_step in range(5):
            for col_step in range(5):
                window = padded[:, depth_step:depth_step + planes, row_step:row_step + tile_x, col_step:col_step + tile_y, :]
                rows_list.append(jnp.sum(window * grad_wide, axis=(0, 1, 2, 3)))
    return jnp.stack(rows_list)


def rounded(value):
    return lax.optimization_barrier(value.astype(jnp.bfloat16)).astype(jnp.float32)


def block_products(left_rows, weight):
    block_size = weight.shape[1] // N_COL

    def add_block(block_index, running):
        first_col = (block_index * block_size).astype(jnp.int32)
        left_piece = lax.dynamic_slice_in_dim(left_rows, first_col, block_size, 1)
        weight_piece = lax.dynamic_slice_in_dim(weight, first_col, block_size, 1)
        product = jnp.dot(left_piece, weight_piece.T, preferred_element_type=jnp.float32)
        return running + rounded(product)

    start_sum = jnp.zeros((left_rows.shape[0], weight.shape[0]), jnp.float32)
    return lax.fori_loop(0, N_COL, add_block, start_sum)


def grouped(field):
    shaped = field.reshape(N_DP, STATES_DEV, N_ROW, PLANES, TILE_X, TILE_Y, field.shape[-1])
    shaped = jnp.transpose(shaped, (0, 2, 1, 3, 4, 5, 6))
    return shaped.reshape(N_DP * N_ROW, STATES_DEV * PLANES * TILE_X * TILE_Y, field.shape[-1])


def group_products(left_field, right_field):
    left_groups = grouped(left_field)
    right_groups = grouped(right_field)

    def add_group(running, pieces):
        product = jnp.dot(pieces[0].T, pieces[1], preferred_element_type=jnp.float32)
        return running + rounded(product), None

    start_sum = jnp.zeros((left_groups.shape[2], right_groups.shape[2]), jnp.float32)
    running, unused = lax.scan(add_group, start_sum, (left_groups, right_groups))
    return running


def reference(inputs, up_weight, down_weight, kernel, cotangent):
    full_width = inputs.shape[4]
    flat_inputs = inputs.reshape(-1, full_width)
    flat_cotangent = cotangent.reshape(-1, full_width)
    field_shape = inputs.shape[:4] + (EXPAND,)
    hidden = jnp.dot(flat_inputs, up_weight, preferred_element_type=jnp.float32).astype(jnp.bfloat16).reshape(field_shape)
    hidden_pad = pad_field(hidden)
    preact = stencil_sum(hidden_pad, kernel, 0, DEPTH, TILE_X, TILE_Y)
    activation = jax.nn.silu(preact).astype(jnp.bfloat16)
    flat_act = activation.reshape(-1, EXPAND)
    block_output = (inputs.astype(jnp.float32) + block_products(flat_act, down_weight).reshape(inputs.shape)).astype(jnp.bfloat16)
    act_grad = jnp.dot(flat_cotangent, down_weight, preferred_element_type=jnp.float32).reshape(field_shape)
    logistic = jax.nn.sigmoid(preact)
    preact_grad = (act_grad * logistic * (1.0 + preact * (1.0 - logistic))).astype(jnp.bfloat16)
    grad_pad = pad_field(preact_grad)
    hidden_grad = stencil_sum(grad_pad, kernel, 1, DEPTH, TILE_X, TILE_Y).astype(jnp.bfloat16)
    kernel_grad = kernel_terms(hidden_pad, preact_grad, DEPTH, TILE_X, TILE_Y)
    flat_grad_hidden = hidden_grad.reshape(-1, EXPAND)
    input_grad = (cotangent.astype(jnp.float32) + block_products(flat_grad_hidden, up_weight).reshape(inputs.shape)).astype(jnp.bfloat16)
    up_grad = group_products(inputs, hidden_grad).astype(jnp.bfloat16)
    down_grad = group_products(cotangent, activation).astype(jnp.bfloat16)
    return (block_output, input_grad, up_grad, down_grad, kernel_grad)
```

```python
import functools

import jax
import jax.numpy as jnp
import ml_dtypes
import numpy as np
from jax import lax
from jax.experimental import pallas as pl
from jax.experimental.pallas import tpu as pltpu
from jax.sharding import PartitionSpec as P

HALO = 2


def aligned(index, size):
    return pl.ds(pl.multiple_of(index * size, size), size)


def transforms(planes, tile_x, tile_y):
    lengths = np.array([planes + 2 * HALO, tile_x + HALO, tile_y + HALO])
    waves = np.stack([m.ravel() for m in np.meshgrid(*map(np.arange, lengths), indexing="ij")], 1)
    mirrored = (-waves) % lengths
    code = waves @ np.array([lengths[1] * lengths[2], lengths[2], 1])
    mirrored_code = mirrored @ np.array([lengths[1] * lengths[2], lengths[2], 1])
    kept = code <= mirrored_code
    waves, weight = waves[kept], np.where(code == mirrored_code, 1.0, 2.0)[kept] / lengths.prod()
    rows = -(-len(waves) // 16) * 16

    def wave_matrix(*ranges):
        points = np.stack([m.ravel() for m in np.meshgrid(*ranges, indexing="ij")], 1)
        angle = 2 * np.pi * (waves / lengths) @ points.T
        both = np.zeros((2, rows, len(points)))
        both[0, : len(waves)], both[1, : len(waves)] = np.cos(angle), -np.sin(angle)
        return both

    weights = np.zeros(rows)
    weights[: len(waves)] = weight

    def forward(both):
        return both.reshape(2 * rows, -1)

    def backward(both):
        return (both * weights[:, None]).reshape(2 * rows, -1).T

    depth, along_x, along_y = np.arange(planes + 2 * HALO), np.arange(tile_x), np.arange(tile_y)
    reach = np.arange(-HALO, HALO + 1)
    grid = wave_matrix(depth, along_x, along_y)
    own = wave_matrix(depth[HALO:-HALO], along_x, along_y)
    taps = wave_matrix(reach, reach, reach)
    bf16 = ml_dtypes.bfloat16
    taps_high = forward(taps).astype(bf16)
    taps_low = (forward(taps) - taps_high.astype(np.float64)).astype(bf16)
    taps_back = backward(taps)
    taps_back = np.concatenate([taps_back, np.zeros((-len(taps_back) % 16, taps_back.shape[1]))])
    return (
        forward(grid).astype(bf16), backward(own).astype(bf16), np.stack([taps_high, taps_low]), taps_back.astype(bf16)
    )


def block_kernel(
    sizes, inputs, cotangent, up_weight, down_weight, stencil_weights, to_waves, from_waves, taps_to_waves, taps_from_waves,
    block_output, input_grad, up_grad, down_grad, kernel_grad,
    kernel, xg, cg, upw, dnw, hid, grd, wide, act, hgr, fwd, inv, fwd_taps, inv_taps, tap_waves, hid_waves, waves, sent, got, turned,
    first_out, first_in, second_out, second_in, taps_out, taps_in, share_out, share_in, half_out, half_in,
    load_sem, ag_s, ag_r, halo_s, halo_r, rs_s, rs_r, pair_s, pair_r, row_s, row_r, kg_s, kg_r,
):
    planes, tile_x, tile_y, n_dp, n_row, n_col = sizes
    dp, row, col = lax.axis_index("dp"), lax.axis_index("row"), lax.axis_index("col")
    partner = {"dp": 1 - dp}
    voxels, local = inputs.shape
    channels = kernel.shape[1]
    plane = tile_x * tile_y
    own = slice(HALO * plane, HALO * plane + voxels)
    tile = min(256, channels)
    wtile = min(256, local)
    n_half = n_col // 2
    share = first_out.shape[1] * local // n_row
    bf16, f32 = jnp.bfloat16, jnp.float32
    mine = aligned(col, local)

    loads = [
        pltpu.make_async_copy(source, target, load_sem.at[i])
        for i, (source, target) in enumerate(
            ((inputs, xg.at[:, mine]), (up_weight, upw), (stencil_weights, kernel), (cotangent, cg.at[:, mine]), (down_weight, dnw),
             (to_waves, fwd), (from_waves, inv), (taps_to_waves, fwd_taps), (taps_from_waves, inv_taps))
        )
    ]
    for load in loads:
        load.start()

    barrier = pltpu.get_barrier_semaphore()

    @pl.loop(1, n_col)
    def _(k):
        pl.semaphore_signal(barrier, inc=1, device_id={"col": lax.rem(col + k, n_col)})

    @pl.loop(1, n_row)
    def _(k):
        pl.semaphore_signal(barrier, inc=1, device_id={"row": lax.rem(row + k, n_row)})

    pl.semaphore_signal(barrier, inc=1, device_id=partner)
    pl.semaphore_wait(barrier, n_col + n_row - 1)

    def remote(source, target, send, receive, device):
        return pltpu.make_async_remote_copy(
            src_ref=source, dst_ref=target, send_sem=send, recv_sem=receive,
            device_id=device, device_id_type=pl.DeviceIdType.MESH,
        )

    def hop(i, side, step):
        gathered = (xg, cg)[i]
        source = (inputs, cotangent)[i] if step == 0 else gathered.at[:, aligned(col - side * step, local)]
        return remote(
            source, gathered.at[:, aligned(col - side * step, local)],
            ag_s.at[i, (side + 1) // 2, step], ag_r.at[i, (side + 1) // 2, step], {"col": col + side},
        )

    def inside(index):
        return jnp.logical_and(index >= 0, index < n_col)

    def hop_start(i, step):
        for side in (1, -1):
            pl.when(jnp.logical_and(inside(col + side), inside(col - side * step)))(hop(i, side, step).start)

    def hop_received(i, step):
        for side in (1, -1):
            pl.when(inside(col - side * (step + 1)))(hop(i, side, step).wait_recv)

    def hop_sent(i, step):
        for side in (1, -1):
            pl.when(jnp.logical_and(inside(col + side), inside(col - side * step)))(hop(i, side, step).wait_send)

    def advance(i, step):
        if step < n_col - 1:
            hop_received(i, step - 1)
            hop_start(i, step)

    def each(count, action, first=1):
        @pl.loop(first, count)
        def _(k):
            action(k)

    hop_start(0, 0)
    loads[2].wait()
    loads[7].wait()

    @pl.loop(0, channels // tile)
    def _(n):
        cols = aligned(n, tile)
        weights = kernel[:, cols]
        high = weights.astype(bf16)
        low = (weights - high.astype(f32)).astype(bf16)
        tap_waves[:, cols] = (
            jnp.dot(fwd_taps[0], high, preferred_element_type=f32)
            + jnp.dot(fwd_taps[1], high, preferred_element_type=f32)
            + jnp.dot(fwd_taps[0], low, preferred_element_type=f32)
        )

    for step in range(1, n_col - 1):
        advance(0, step)
    hop_start(1, 0)
    hop_received(0, n_col - 2)
    loads[0].wait()
    loads[1].wait()

    @pl.loop(0, channels // tile)
    def _(n):
        cols = aligned(n, tile)
        hid[own, cols] = jnp.dot(xg[...], upw[:, cols], preferred_element_type=f32).astype(bf16)

    def turn(i, left):
        @pl.loop(0, n_col)
        def _(chunk):
            turned[i, aligned(chunk, local)] = left[:, aligned(chunk, local)].T

    def halo(i, field, side):
        if side:
            source, target, peer = field.at[HALO * plane : 2 * HALO * plane], voxels + HALO * plane, row - 1
        else:
            source, target, peer = field.at[voxels : voxels + HALO * plane], 0, row + 1
        return remote(
            source, field.at[target : target + HALO * plane], halo_s.at[i, side], halo_r.at[i, side], {"row": peer}
        )

    def halo_start(i, field):
        @pl.when(row < n_row - 1)
        def _():
            halo(i, field, 0).start()

        @pl.when(row > 0)
        def _():
            halo(i, field, 1).start()

        @pl.when(row == 0)
        def _():
            field[0 : HALO * plane] = jnp.zeros((HALO * plane, channels), bf16)

        @pl.when(row == n_row - 1)
        def _():
            field[voxels + HALO * plane :] = jnp.zeros((HALO * plane, channels), bf16)

    def halo_wait(i, field):
        @pl.when(row > 0)
        def _():
            halo(i, field, 0).wait_recv()
            halo(i, field, 1).wait_send()

        @pl.when(row < n_row - 1)
        def _():
            halo(i, field, 1).wait_recv()
            halo(i, field, 0).wait_send()

    halo_start(0, hid)
    advance(1, 1)
    turn(0, xg)
    loads[5].wait()
    loads[6].wait()
    halo_wait(0, hid)
    half_waves = tap_waves.shape[0] // 2

    def split(array, cols):
        return array[0:half_waves, cols], array[half_waves : 2 * half_waves, cols]

    def product(left, right, conjugate):
        if conjugate:
            return jnp.concatenate([left[0] * right[0] + left[1] * right[1], left[1] * right[0] - left[0] * right[1]])
        return jnp.concatenate([left[0] * right[0] - left[1] * right[1], left[1] * right[0] + left[0] * right[1]])

    @pl.loop(0, channels // tile)
    def _(n):
        cols = aligned(n, tile)
        hid_waves[:, cols] = jnp.dot(fwd[...], hid[:, cols], preferred_element_type=f32)
        pre_waves = product(split(hid_waves, cols), split(tap_waves, cols), True).astype(bf16)
        preact = jnp.dot(inv[...], pre_waves, preferred_element_type=f32)
        wide[:, cols] = preact
        act[:, cols] = (preact * jax.nn.sigmoid(preact)).astype(bf16)

    advance(1, 2)

    loads[3].wait()
    loads[4].wait()
    for step in range(3, n_col - 1):
        advance(1, step)
    hop_received(1, n_col - 2)

    @pl.loop(0, channels // tile)
    def _(n):
        cols = aligned(n, tile)
        act_grad = jnp.dot(cg[...], dnw[:, cols], preferred_element_type=f32)
        preact = wide[:, cols]
        logistic = jax.nn.sigmoid(preact)
        grd[own, cols] = (act_grad * logistic * (1.0 + preact * (1.0 - logistic))).astype(bf16)

    halo_start(1, grd)

    def pair(i, j):
        return remote(first_out.at[i, j], first_in.at[i, j], pair_s.at[i, j], pair_r.at[i, j], partner)

    def grad_for_partner(i, right):
        @pl.loop(0, n_half)
        def _(j):
            chunk = aligned((1 - dp) * n_half + j, local)

            @pl.loop(0, channels // tile)
            def _(n):
                cols = aligned(n, tile)
                first_out[i, j, :, cols] = jnp.dot(
                    turned[1 - i, chunk], right[:, cols], preferred_element_type=f32
                ).astype(bf16)

            pair(i, j).start()

    def row_copy(i, k):
        peer = lax.rem(row + k, n_row)
        return remote(
            second_out.at[i, aligned(peer, share)], second_in.at[i, k], row_s.at[i, k], row_r.at[i, k], {"row": peer}
        )

    def grad_own(i, right):
        @pl.loop(0, n_half)
        def _(j):
            chunk = aligned(dp * n_half + j, local)
            pair(i, j).wait_recv()

            @pl.loop(0, channels // tile)
            def _(n):
                cols = aligned(n, tile)
                product = jnp.dot(turned[1 - i, chunk], right[:, cols], preferred_element_type=f32).astype(bf16)
                both = product.astype(f32) + first_in[i, j, :, cols].astype(f32)
                second_out[i, aligned(j, local), cols] = both.astype(bf16)

            for part in range(local // share):
                peer = j * (local // share) + part
                k = lax.rem(peer - row + n_row, n_row)
                pl.when(peer != row)(lambda: row_copy(i, k).start())

    def grad_finish(i, out):
        each(n_row, lambda k: row_copy(i, k).wait_recv())

        @pl.loop(0, channels // tile)
        def _(n):
            cols = aligned(n, tile)
            total = second_out[i, aligned(row, share), cols].astype(f32)
            for k in range(1, n_row):
                total = total + second_in[i, k, :, cols].astype(f32)
            out[:, cols] = total.astype(bf16)

        each(n_row, lambda k: row_copy(i, k).wait_send())
        each(n_half, lambda j: pair(i, j).wait_send(), 0)

    def column_copy(i, k):
        return remote(sent.at[i, k], got.at[i, k], rs_s.at[i, k], rs_r.at[i, k], {"col": lax.rem(col + k, n_col)})

    def column_partials(i, left, weight):
        def one(k):
            first = lax.rem(col + k, n_col) * local

            @pl.loop(0, local // wtile)
            def _(n):
                rows = pl.ds(pl.multiple_of(first + n * wtile, wtile), wtile)
                product = lax.dot_general(
                    left[...], weight[rows, :], (((1,), (1,)), ((), ())), preferred_element_type=f32
                )
                sent[i, k, :, aligned(n, wtile)] = product.astype(bf16)

        @pl.loop(1, n_col)
        def _(k):
            one(k)
            column_copy(i, k).start()

        one(0)

    def column_finish(i, residual, out):
        each(n_col, lambda k: column_copy(i, k).wait_recv())
        total = sent[i, 0].astype(f32)
        for k in range(1, n_col):
            total = total + got[i, k].astype(f32)
        out[...] = (residual[:, mine].astype(f32) + total).astype(bf16)
        each(n_col, lambda k: column_copy(i, k).wait_send())

    turn(1, cg)
    grad_for_partner(0, act)
    column_partials(0, act, dnw)
    grad_own(0, act)
    halo_wait(1, grd)

    @pl.loop(0, channels // tile)
    def _(n):
        cols = aligned(n, tile)
        grd_waves = jnp.dot(fwd[...], grd[:, cols], preferred_element_type=f32)
        waves[:, 0:tile] = grd_waves
        back_waves = product(split(waves, slice(0, tile)), split(tap_waves, cols), False).astype(bf16)
        hgr[:, cols] = jnp.dot(inv[...], back_waves, preferred_element_type=f32).astype(bf16)

    grad_for_partner(1, hgr)
    column_partials(1, hgr, upw)
    grad_own(1, hgr)
    loads[8].wait()

    @pl.loop(0, channels // tile)
    def _(n):
        cols = aligned(n, tile)
        waves[:, 0:tile] = jnp.dot(fwd[:, own], grd[own, cols], preferred_element_type=f32)
        sum_waves = product(split(hid_waves, cols), split(waves, slice(0, tile)), True).astype(bf16)
        taps_out[:, cols] = jnp.dot(inv_taps[...], sum_waves, preferred_element_type=f32).astype(bf16)

    whole_taps = remote(taps_out, taps_in, kg_s.at[0], kg_r.at[0], partner)
    whole_taps.start()
    column_finish(0, xg, block_output)
    whole_taps.wait_recv()
    some = aligned(dp, channels // 2)
    share_out[...] = (taps_out[:, some].astype(f32) + taps_in[:, some].astype(f32)).astype(bf16)

    def taps_copy(k):
        return remote(share_out, share_in.at[k], kg_s.at[k], kg_r.at[k], {"row": lax.rem(row + k, n_row)})

    each(n_row, lambda k: taps_copy(k).start())
    grad_finish(0, down_grad)
    column_finish(1, cg, input_grad)
    each(n_row, lambda k: taps_copy(k).wait_recv())
    total = share_out[...].astype(f32)
    for k in range(1, n_row):
        total = total + share_in[k].astype(f32)
    half_out[...] = total
    halves = remote(half_out, half_in, kg_s.at[n_row], kg_r.at[n_row], partner)
    halves.start()
    kernel_grad[:, some] = half_out[0 : kernel.shape[0]]
    grad_finish(1, up_grad)
    halves.wait_recv()
    kernel_grad[:, aligned(1 - dp, channels // 2)] = half_in[0 : kernel.shape[0]]
    for i in range(2):
        for step in range(n_col - 1):
            hop_sent(i, step)
    whole_taps.wait_send()
    each(n_row, lambda k: taps_copy(k).wait_send())
    halves.wait_send()


def hand_on(*refs):
    arrived, done = refs[15], refs[16]
    fetches = [pltpu.make_async_copy(refs[i], refs[10 + i], arrived.at[i]) for i in range(5)]
    stores = [pltpu.make_async_copy(refs[10 + i], refs[5 + i], done.at[i]) for i in range(5)]
    for fetch in fetches:
        fetch.start()
    for fetch, store in zip(fetches, stores):
        fetch.wait()
        store.start()
    for store in stores:
        store.wait()


def on_device(inputs, up_weight, down_weight, kernel, cotangent):
    _, planes, tile_x, tile_y, local = inputs.shape
    n_dp, n_row, n_col = (lax.axis_size(name) for name in ("dp", "row", "col"))
    voxels = planes * tile_x * tile_y
    extended = voxels + 2 * HALO * tile_x * tile_y
    width, channels = up_weight.shape
    share = width // (n_dp * n_row)
    bf16, f32 = jnp.bfloat16, jnp.float32
    dma = pltpu.SemaphoreType.DMA
    taps = kernel.shape[0]
    tap_rows = -(-taps // 16) * 16
    vmem, anywhere = pl.BlockSpec(memory_space=pltpu.VMEM), pl.BlockSpec(memory_space=pl.ANY)
    matrices = transforms(planes, tile_x, tile_y)
    n_waves = matrices[0].shape[0]
    outs = pl.pallas_call(
        functools.partial(block_kernel, (planes, tile_x, tile_y, n_dp, n_row, n_col)),
        out_shape=(
            jax.ShapeDtypeStruct((voxels, local), bf16),
            jax.ShapeDtypeStruct((voxels, local), bf16),
            jax.ShapeDtypeStruct((share, channels), bf16),
            jax.ShapeDtypeStruct((share, channels), bf16),
            jax.ShapeDtypeStruct((taps, channels), f32),
        ),
        in_specs=[anywhere] * 9,
        out_specs=(vmem,) * 5,
        scratch_shapes=[
            pltpu.VMEM(kernel.shape, f32),
            pltpu.VMEM((voxels, width), bf16),
            pltpu.VMEM((voxels, width), bf16),
            pltpu.VMEM((width, channels), bf16),
            pltpu.VMEM((width, channels), bf16),
            pltpu.VMEM((extended, channels), bf16),
            pltpu.VMEM((extended, channels), bf16),
            pltpu.VMEM((voxels, channels), f32),
            pltpu.VMEM((voxels, channels), bf16),
            pltpu.VMEM((voxels, channels), bf16),
            *(pltpu.VMEM(m.shape, bf16) for m in matrices),
            pltpu.VMEM((n_waves, channels), f32),
            pltpu.VMEM((n_waves, channels), f32),
            pltpu.VMEM((n_waves, min(256, channels)), f32),
            pltpu.VMEM((2, n_col, voxels, local), bf16),
            pltpu.VMEM((2, n_col, voxels, local), bf16),
            pltpu.VMEM((2, width, voxels), bf16),
            pltpu.VMEM((2, n_col // 2, local, channels), bf16),
            pltpu.VMEM((2, n_col // 2, local, channels), bf16),
            pltpu.VMEM((2, width // 2, channels), bf16),
            pltpu.VMEM((2, n_row, share, channels), bf16),
            pltpu.VMEM((tap_rows, channels), bf16),
            pltpu.VMEM((tap_rows, channels), bf16),
            pltpu.VMEM((tap_rows, channels // 2), bf16),
            pltpu.VMEM((n_row, tap_rows, channels // 2), bf16),
            pltpu.VMEM((tap_rows, channels // 2), f32),
            pltpu.VMEM((tap_rows, channels // 2), f32),
            dma((9,)),
            dma((2, 2, n_col)), dma((2, 2, n_col)),
            dma((2, 2)), dma((2, 2)),
            dma((2, n_col)), dma((2, n_col)),
            dma((2, n_col // 2)), dma((2, n_col // 2)),
            dma((2, n_row)), dma((2, n_row)),
            dma((n_row + 1,)), dma((n_row + 1,)),
        ],
        compiler_params=pltpu.CompilerParams(
            collective_id=0, has_side_effects=True, vmem_limit_bytes=56 << 20
        ),
    )(inputs.reshape(voxels, local), cotangent.reshape(voxels, local), up_weight, down_weight, kernel,
      *map(jnp.asarray, matrices))
    outs = pl.pallas_call(
        hand_on,
        out_shape=tuple(jax.ShapeDtypeStruct(out.shape, out.dtype) for out in outs),
        in_specs=[anywhere] * 5,
        out_specs=(anywhere,) * 5,
        scratch_shapes=[pltpu.VMEM(out.shape, out.dtype) for out in outs] + [dma((5,)), dma((5,))],
    )(*outs)
    return (outs[0].reshape(inputs.shape), outs[1].reshape(inputs.shape)) + tuple(outs[2:])


def solution(mesh):
    placed = (
        P("dp", "row", None, None, "col"),
        P(None, "col"),
        P(None, "col"),
        P(None, "col"),
        P("dp", "row", None, None, "col"),
    )
    return jax.shard_map(
        on_device,
        mesh=mesh,
        in_specs=placed,
        out_specs=(
            P("dp", "row", None, None, "col"),
            P("dp", "row", None, None, "col"),
            P(("dp", "row"), "col"),
            P(("dp", "row"), "col"),
            P(None, "col"),
        ),
        check_vma=False,
    )
```

```python
import functools

import jax
import jax.numpy as jnp
import ml_dtypes
import numpy as np
from jax import lax
from jax.experimental import pallas as pl
from jax.experimental.pallas import tpu as pltpu
from jax.sharding import PartitionSpec as P

HALO = 2


def aligned(index, size):
    return pl.ds(pl.multiple_of(index * size, size), size)


def transforms(planes, tile_x, tile_y):
    lengths = np.array([planes + 2 * HALO, tile_x + HALO, tile_y + HALO])
    waves = np.stack([m.ravel() for m in np.meshgrid(*map(np.arange, lengths), indexing="ij")], 1)
    mirrored = (-waves) % lengths
    code = waves @ np.array([lengths[1] * lengths[2], lengths[2], 1])
    mirrored_code = mirrored @ np.array([lengths[1] * lengths[2], lengths[2], 1])
    kept = code <= mirrored_code
    waves, weight = waves[kept], np.where(code == mirrored_code, 1.0, 2.0)[kept] / lengths.prod()
    rows = -(-len(waves) // 16) * 16

    def wave_matrix(*ranges):
        points = np.stack([m.ravel() for m in np.meshgrid(*ranges, indexing="ij")], 1)
        angle = 2 * np.pi * (waves / lengths) @ points.T
        both = np.zeros((2, rows, len(points)))
        both[0, : len(waves)], both[1, : len(waves)] = np.cos(angle), -np.sin(angle)
        return both

    weights = np.zeros(rows)
    weights[: len(waves)] = weight

    def forward(both):
        return both.reshape(2 * rows, -1)

    def backward(both):
        return (both * weights[:, None]).reshape(2 * rows, -1).T

    depth, along_x, along_y = np.arange(planes + 2 * HALO), np.arange(tile_x), np.arange(tile_y)
    reach = np.arange(-HALO, HALO + 1)
    grid = wave_matrix(depth, along_x, along_y)
    own = wave_matrix(depth[HALO:-HALO], along_x, along_y)
    taps = wave_matrix(reach, reach, reach)
    bf16 = ml_dtypes.bfloat16
    taps_high = forward(taps).astype(bf16)
    taps_low = (forward(taps) - taps_high.astype(np.float64)).astype(bf16)
    taps_back = backward(taps)
    taps_back = np.concatenate([taps_back, np.zeros((-len(taps_back) % 16, taps_back.shape[1]))])
    edge = HALO * tile_x * tile_y
    to_waves = forward(grid)
    return tuple(
        m.astype(bf16)
        for m in (
            to_waves[:, edge:-edge], np.concatenate([to_waves[:, :edge], to_waves[:, -edge:]], 1),
            backward(own), np.stack([taps_high, taps_low]), taps_back,
        )
    )


def block_kernel(
    sizes, inputs, cotangent, up_weight, down_weight, stencil_weights,
    own_to_waves, halo_to_waves, from_waves, taps_to_waves, taps_from_waves,
    block_output, input_grad, up_grad, down_grad, kernel_grad,
    kernel, xg, cg, upw, dnw, hid, grd, hid_halo, grd_halo, wide, right, right_in,
    fwd_own, fwd_halo, inv, fwd_taps, inv_taps, tap_waves, hid_waves, grd_waves,
    sent, got, own_sum, turned, turned_in, first_out, first_in, second_out, second_in,
    taps_out, taps_in, share_out, share_in, half_out, half_in,
    load_sem, ag_s, ag_r, cot_s, cot_r, halo_s, halo_r, chain_s, chain_r, piece_s, piece_r,
    gather_s, gather_r, pair_s, pair_r, row_s, row_r, kg_s, kg_r,
):
    planes, tile_x, tile_y, n_dp, n_row, n_col = sizes
    dp, row, col = lax.axis_index("dp"), lax.axis_index("row"), lax.axis_index("col")
    partner = {"dp": 1 - dp}
    voxels, local = inputs.shape
    channels = kernel.shape[1]
    edge = HALO * tile_x * tile_y
    tile = min(256, channels)
    n_tiles = channels // tile
    wtile = min(256, local)
    parts = ag_s.shape[2]
    part_rows = voxels // parts
    n_half = n_row // 2
    share = first_out.shape[2]
    bf16, f32 = jnp.bfloat16, jnp.float32
    mine = aligned(col, local)
    act, hgr = right.at[0], right.at[1]

    loads = [
        pltpu.make_async_copy(source, target, load_sem.at[i])
        for i, (source, target) in enumerate((
            (inputs, xg.at[:, mine]), (up_weight, upw), (stencil_weights, kernel), (cotangent, cg.at[:, mine]),
            (down_weight, dnw), (own_to_waves, fwd_own), (halo_to_waves, fwd_halo), (from_waves, inv),
            (taps_to_waves, fwd_taps), (taps_from_waves, inv_taps),
        ))
    ]
    for i in (0, 2, 8, 1, 5, 6, 7, 3, 4, 9):
        loads[i].start()

    barrier = pltpu.get_barrier_semaphore()

    for side in (1, -1):
        @pl.when(jnp.logical_and(col + side >= 0, col + side < n_col))
        def _():
            pl.semaphore_signal(barrier, inc=1, device_id={"col": col + side})

    @pl.loop(1, n_row)
    def _(k):
        pl.semaphore_signal(barrier, inc=1, device_id={"row": lax.rem(row + k, n_row)})

    pl.semaphore_signal(barrier, inc=1, device_id=partner)
    ends = jnp.where(col == 0, 1, 0) + jnp.where(col == n_col - 1, 1, 0)
    pl.semaphore_wait(barrier, n_row + 2 - ends)

    def remote(source, target, send, receive, device):
        return pltpu.make_async_remote_copy(
            src_ref=source, dst_ref=target, send_sem=send, recv_sem=receive,
            device_id=device, device_id_type=pl.DeviceIdType.MESH,
        )

    def each(count, action, first=0):
        @pl.loop(first, count)
        def _(k):
            action(k)

    def inside(index):
        return jnp.logical_and(index >= 0, index < n_col)

    def hop(side, step, part):
        rows = slice(part * part_rows, (part + 1) * part_rows)
        place = xg.at[rows, aligned(col - side * step, local)]
        return remote(
            inputs.at[rows] if step == 0 else place, place,
            ag_s.at[(side + 1) // 2, step, part], ag_r.at[(side + 1) // 2, step, part], {"col": col + side},
        )

    def hop_goes(side, step):
        return jnp.logical_and(inside(col + side), inside(col - side * step))

    def hop_start(step, part):
        for side in (1, -1):
            pl.when(hop_goes(side, step))(hop(side, step, part).start)

    def hop_received(step, part):
        for side in (1, -1):
            pl.when(inside(col - side * (step + 1)))(hop(side, step, part).wait_recv)

    def cot_copy(peer, source):
        return remote(cotangent, cg.at[:, aligned(source, local)], cot_s.at[peer], cot_r.at[source], {"col": peer})

    def cot_start(slot):
        pl.when(slot > col)(lambda: cot_copy(slot, col).start())
        pl.when(n_col - 1 - slot < col)(lambda: cot_copy(n_col - 1 - slot, col).start())

    def side_of(i, r):
        return r // n_half if i == 0 else lax.rem(r, 2)

    def place_of(i, r):
        return lax.rem(r, n_half) if i == 0 else r // 2

    def row_of(i, side, place):
        return side * n_half + place if i == 0 else 2 * place + side

    def mate(i):
        return {"row": row_of(i, 1 - side_of(i, row), place_of(i, row))}

    def piece(i, index):
        slot = (index // n_row) * n_half + place_of(i, lax.rem(index, n_row))
        return remote(
            turned.at[i, aligned(index, share)], turned_in.at[i, slot], piece_s.at[i, slot], piece_r.at[i, slot], mate(i)
        )

    def leaves(i, index):
        return side_of(i, lax.rem(index, n_row)) != side_of(i, row)

    def turn(i, field, shard):
        turned[i, aligned(shard, local)] = field[:, aligned(shard, local)].T
        for k in range(local // share):
            index = shard * (local // share) + k
            pl.when(leaves(i, index))(lambda: piece(i, index).start())

    for part in range(parts):
        hop_start(0, part)

    def zero_edges(side):
        for halo in (hid_halo, grd_halo):
            halo[side * edge : (side + 1) * edge] = jnp.zeros((edge, channels), bf16)

    pl.when(row == 0)(lambda: zero_edges(0))
    pl.when(row == n_row - 1)(lambda: zero_edges(1))
    loads[2].wait()
    loads[8].wait()

    @pl.loop(0, n_tiles)
    def _(n):
        cols = aligned(n, tile)
        weights = kernel[:, cols]
        high = weights.astype(bf16)
        low = (weights - high.astype(f32)).astype(bf16)
        tap_waves[:, cols] = (
            jnp.dot(fwd_taps[0], high, preferred_element_type=f32)
            + jnp.dot(fwd_taps[1], high, preferred_element_type=f32)
            + jnp.dot(fwd_taps[0], low, preferred_element_type=f32)
        )

    loads[0].wait()
    loads[1].wait()

    def expand(shard, cols):
        return jnp.dot(xg[:, aligned(shard, local)], upw[aligned(shard, local), cols], preferred_element_type=f32)

    @pl.loop(0, n_tiles)
    def _(n):
        cols = aligned(n, tile)
        wide[:, cols] = expand(col, cols)

    turn(1, xg, col)
    for slot in range(1, n_col - 1):
        for part in range(parts):
            hop_received(slot - 1, part)
            hop_start(slot, part)
        cot_start(slot)
        for side in (1, -1):
            shard = col - side * slot

            @pl.when(inside(shard))
            def _():
                @pl.loop(0, n_tiles)
                def _(n):
                    cols = aligned(n, tile)
                    wide[:, cols] = wide[:, cols] + expand(shard, cols)

                turn(1, xg, shard)

    for part in range(parts):
        hop_received(n_col - 2, part)
    cot_start(n_col - 1)
    last = n_col - 1 - col
    at_end = jnp.logical_or(col == 0, last == 0)

    def halo(i, field, edges, side, cols, n):
        if side:
            source, target, peer = 0, edge, row - 1
        else:
            source, target, peer = voxels - edge, 0, row + 1
        return remote(
            field.at[source : source + edge, cols], edges.at[target : target + edge, cols],
            halo_s.at[i, side, n], halo_r.at[i, side, n], {"row": peer},
        )

    def halo_start(i, field, edges, cols, n):
        pl.when(row < n_row - 1)(lambda: halo(i, field, edges, 0, cols, n).start())
        pl.when(row > 0)(lambda: halo(i, field, edges, 1, cols, n).start())

    def halo_received(i, field, edges, cols, n):
        pl.when(row > 0)(lambda: halo(i, field, edges, 0, cols, n).wait_recv())
        pl.when(row < n_row - 1)(lambda: halo(i, field, edges, 1, cols, n).wait_recv())

    def halo_sent(i, field, edges, cols, n):
        pl.when(row < n_row - 1)(lambda: halo(i, field, edges, 0, cols, n).wait_send())
        pl.when(row > 0)(lambda: halo(i, field, edges, 1, cols, n).wait_send())

    def gather(i, cols, n):
        return remote(
            right.at[i, :, cols], right_in.at[i, :, cols], gather_s.at[i, n], gather_r.at[i, n], mate(i)
        )

    @pl.loop(0, n_tiles)
    def _(n):
        cols = aligned(n, tile)

        @pl.when(at_end)
        def _():
            wide[:, cols] = wide[:, cols] + expand(last, cols)

        hid[:, cols] = wide[:, cols].astype(bf16)
        halo_start(0, hid, hid_halo, cols, n)

    for i in (5, 6, 7):
        loads[i].wait()

    def waves_of(matrix, field, cols):
        return jnp.dot(matrix[...], field[:, cols], preferred_element_type=f32)

    def own_waves(waves, field, cols):
        waves[:, cols] = waves_of(fwd_own, field, cols)

    each(n_tiles, lambda n: own_waves(hid_waves, hid, aligned(n, tile)))

    pl.when(at_end)(lambda: turn(1, xg, last))

    half_waves = tap_waves.shape[0] // 2

    def product(left, other, cols, conjugate):
        lr, li = left[0:half_waves, cols], left[half_waves : 2 * half_waves, cols]
        rr, ri = other[0:half_waves, cols], other[half_waves : 2 * half_waves, cols]
        if conjugate:
            return jnp.concatenate([(lr * rr + li * ri).astype(bf16), (li * rr - lr * ri).astype(bf16)])
        return jnp.concatenate([(lr * rr - li * ri).astype(bf16), (li * rr + lr * ri).astype(bf16)])

    @pl.loop(0, n_tiles)
    def _(n):
        cols = aligned(n, tile)
        halo_received(0, hid, hid_halo, cols, n)
        hid_waves[:, cols] = hid_waves[:, cols] + waves_of(fwd_halo, hid_halo, cols)
        preact = jnp.dot(inv[...], product(hid_waves, tap_waves, cols, True), preferred_element_type=f32)
        wide[:, cols] = preact
        act[:, cols] = (preact * jax.nn.sigmoid(preact)).astype(bf16)
        gather(0, cols, n).start()

    def project(left, weight, dest, out):
        @pl.loop(0, local // wtile)
        def _(n):
            rows = pl.ds(pl.multiple_of(dest * local + n * wtile, wtile), wtile)
            out[:, aligned(n, wtile)] = lax.dot_general(
                left[...], weight[rows, :], (((1,), (1,)), ((), ())), preferred_element_type=f32
            ).astype(out.dtype)

    def chain(i, side, dest, part):
        rows = aligned(part, part_rows)
        return remote(
            sent.at[i, side, dest, rows], got.at[i, side, dest, rows], chain_s.at[i, side, dest, part],
            chain_r.at[i, side, dest, part], {"col": col - 1 if side else col + 1},
        )

    def chains(m):
        far = n_col - 1 - m
        return ((0, far, far > col, col == 0), (1, m, m < col, col == n_col - 1))

    def chain_begin(i, left, weight):
        @pl.loop(0, n_col - 1)
        def _(m):
            for side, dest, goes, first in chains(m):
                @pl.when(goes)
                def _():
                    project(left, weight, dest, sent.at[i, side, dest])

                    @pl.when(first)
                    def _():
                        for part in range(parts):
                            chain(i, side, dest, part).start()

    def chain_add(i, m, part):
        rows = aligned(part, part_rows)
        for side, dest, goes, first in chains(m):
            @pl.when(jnp.logical_and(goes, jnp.logical_not(first)))
            def _():
                chain(i, side, dest, part).wait_recv()
                total = sent[i, side, dest, rows].astype(f32) + got[i, side, dest, rows].astype(f32)
                sent[i, side, dest, rows] = total.astype(bf16)
                chain(i, side, dest, part).start()

    def chain_end(i, residual, out):
        for part in range(parts):
            rows = slice(part * part_rows, (part + 1) * part_rows)
            for side, arrives in ((0, col > 0), (1, col < n_col - 1)):
                @pl.when(arrives)
                def _():
                    chain(i, side, col, part).wait_recv()
                    own_sum[i, rows] = own_sum[i, rows] + got[i, side, col, rows].astype(f32)

            out[rows] = (residual[rows, mine].astype(f32) + own_sum[i, rows]).astype(bf16)

    def chain_sent(i, m):
        for side, dest, goes, _ in chains(m):
            @pl.when(goes)
            def _():
                for part in range(parts):
                    chain(i, side, dest, part).wait_send()

    loads[4].wait()
    chain_begin(0, act, dnw)
    loads[3].wait()

    @pl.loop(0, n_col)
    def _(k):
        pl.when(k != col)(lambda: cot_copy(col, k).wait_recv())

    @pl.loop(0, n_tiles)
    def _(n):
        cols = aligned(n, tile)
        act_grad = jnp.dot(cg[...], dnw[:, cols], preferred_element_type=f32)
        preact = wide[:, cols]
        logistic = jax.nn.sigmoid(preact)
        grd[:, cols] = (act_grad * logistic * (1.0 + preact * (1.0 - logistic))).astype(bf16)
        halo_start(1, grd, grd_halo, cols, n)

    each(n_tiles, lambda n: own_waves(grd_waves, grd, aligned(n, tile)))
    loads[9].wait()

    @pl.loop(0, n_tiles)
    def _(n):
        cols = aligned(n, tile)
        taps_out[:, cols] = jnp.dot(
            inv_taps[...], product(hid_waves, grd_waves, cols, True), preferred_element_type=f32
        ).astype(bf16)

    whole_taps = remote(taps_out, taps_in, kg_s.at[0], kg_r.at[0], partner)
    whole_taps.start()
    each(n_col, lambda k: turn(0, cg, k))
    project(act, dnw, col, own_sum.at[0])
    for part in range(parts):
        chain_add(0, 0, part)

    @pl.loop(0, n_tiles)
    def _(n):
        cols = aligned(n, tile)
        halo_received(1, grd, grd_halo, cols, n)
        grd_waves[:, cols] = grd_waves[:, cols] + waves_of(fwd_halo, grd_halo, cols)
        hgr[:, cols] = jnp.dot(
            inv[...], product(grd_waves, tap_waves, cols, False), preferred_element_type=f32
        ).astype(bf16)
        gather(1, cols, n).start()

    chain_begin(1, hgr, upw)

    def pair(i, j, cols, n):
        return remote(first_out.at[i, j, :, cols], first_in.at[i, j, :, cols], pair_s.at[i, j, n], pair_r.at[i, j, n], partner)

    def row_copy(i, to, source, cols, n):
        return remote(
            second_out.at[i, to, :, cols], second_in.at[i, source, :, cols], row_s.at[i, to, n], row_r.at[i, source, n],
            {"row": row_of(i, side_of(i, row), to)},
        )

    def outer(i, half, j, cols):
        index = half * n_row + row_of(i, side_of(i, row), j)
        return jnp.dot(
            turned[i, aligned(index, share)], right[i, :, cols], preferred_element_type=f32
        ) + jnp.dot(turned_in[i, half * n_half + j], right_in[i, :, cols], preferred_element_type=f32)

    def grad_for_partner(i, n):
        cols = aligned(n, tile)
        gather(i, cols, n).wait_recv()

        @pl.loop(0, n_half)
        def _(j):
            first_out[i, j, :, cols] = outer(i, 1 - dp, j, cols).astype(bf16)
            pair(i, j, cols, n).start()

    def grad_own(i, n):
        cols = aligned(n, tile)
        here = place_of(i, row)

        @pl.loop(0, n_half)
        def _(j):
            total = outer(i, dp, j, cols)
            pair(i, j, cols, n).wait_recv()
            second_out[i, j, :, cols] = (total + first_in[i, j, :, cols].astype(f32)).astype(bf16)
            pl.when(j != here)(lambda: row_copy(i, j, here, cols, n).start())

    def grad_step(i, step):
        pl.when(step < n_tiles)(lambda: grad_for_partner(i, step))
        pl.when(jnp.logical_and(step > 0, step <= n_tiles))(lambda: grad_own(i, step - 1))

    def grad_finish(i, out):
        here = place_of(i, row)

        @pl.loop(0, n_tiles)
        def _(n):
            cols = aligned(n, tile)
            own_sum_tile = second_out[i, here, :, cols].astype(f32)
            for k in range(1, n_half):
                source = lax.rem(here + k, n_half)
                row_copy(i, here, source, cols, n).wait_recv()
                own_sum_tile = own_sum_tile + second_in[i, source, :, cols].astype(f32)
            out[:, cols] = own_sum_tile.astype(bf16)

    def pieces_received(i):
        @pl.loop(0, n_dp * n_half)
        def _(slot):
            index = (slot // n_half) * n_row + row_of(i, 1 - side_of(i, row), lax.rem(slot, n_half))
            piece(i, index).wait_recv()

    pieces_received(0)
    each(n_tiles + 1, lambda step: grad_step(0, step))
    for m in range(1, n_col - 1):
        for part in range(parts):
            chain_add(0, m, part)
    chain_end(0, xg, block_output)

    whole_taps.wait_recv()
    some = aligned(dp, channels // 2)
    share_out[...] = (taps_out[:, some].astype(f32) + taps_in[:, some].astype(f32)).astype(bf16)

    def taps_copy(k):
        return remote(share_out, share_in.at[k], kg_s.at[k], kg_r.at[k], {"row": lax.rem(row + k, n_row)})

    each(n_row, lambda k: taps_copy(k).start(), 1)
    project(hgr, upw, col, own_sum.at[1])
    pieces_received(1)
    n_adds = (n_col - 1) * parts

    @pl.loop(0, max(n_tiles + 1, n_adds))
    def _(step):
        grad_step(1, step)
        pl.when(step < n_adds)(lambda: chain_add(1, step // parts, lax.rem(step, parts)))

    grad_finish(0, down_grad)
    each(n_row, lambda k: taps_copy(k).wait_recv(), 1)
    total = share_out[...].astype(f32)
    for k in range(1, n_row):
        total = total + share_in[k].astype(f32)
    half_out[...] = total
    halves = remote(half_out, half_in, kg_s.at[n_row], kg_r.at[n_row], partner)
    halves.start()
    kernel_grad[:, some] = half_out[0 : kernel.shape[0]]
    grad_finish(1, up_grad)
    halves.wait_recv()
    kernel_grad[:, aligned(1 - dp, channels // 2)] = half_in[0 : kernel.shape[0]]
    chain_end(1, cg, input_grad)

    for step in range(n_col - 1):
        for part in range(parts):
            for side in (1, -1):
                pl.when(hop_goes(side, step))(hop(side, step, part).wait_send)
    each(n_col, lambda k: pl.when(k != col)(lambda: cot_copy(k, col).wait_send()))
    for i in range(2):
        each(n_col - 1, lambda m: chain_sent(i, m))
        each(n_dp * n_row, lambda k: pl.when(leaves(i, k))(lambda: piece(i, k).wait_send()))

        @pl.loop(0, n_tiles)
        def _(n):
            cols = aligned(n, tile)
            halo_sent(i, (hid, grd)[i], (hid_halo, grd_halo)[i], cols, n)
            gather(i, cols, n).wait_send()
            here = place_of(i, row)
            for j in range(n_half):
                pair(i, j, cols, n).wait_send()
                pl.when(j != here)(lambda: row_copy(i, j, here, cols, n).wait_send())

    whole_taps.wait_send()
    each(n_row, lambda k: taps_copy(k).wait_send(), 1)
    halves.wait_send()


def hand_on(*refs):
    arrived, done = refs[15], refs[16]
    fetches = [pltpu.make_async_copy(refs[i], refs[10 + i], arrived.at[i]) for i in range(5)]
    stores = [pltpu.make_async_copy(refs[10 + i], refs[5 + i], done.at[i]) for i in range(5)]
    for fetch in fetches:
        fetch.start()
    for fetch, store in zip(fetches, stores):
        fetch.wait()
        store.start()
    for store in stores:
        store.wait()


def on_device(inputs, up_weight, down_weight, kernel, cotangent):
    _, planes, tile_x, tile_y, local = inputs.shape
    n_dp, n_row, n_col = (lax.axis_size(name) for name in ("dp", "row", "col"))
    voxels = planes * tile_x * tile_y
    extended = voxels + 2 * HALO * tile_x * tile_y
    width, channels = up_weight.shape
    share = width // (n_dp * n_row)
    bf16, f32 = jnp.bfloat16, jnp.float32
    dma = pltpu.SemaphoreType.DMA
    taps = kernel.shape[0]
    tap_rows = -(-taps // 16) * 16
    vmem, anywhere = pl.BlockSpec(memory_space=pltpu.VMEM), pl.BlockSpec(memory_space=pl.ANY)
    matrices = transforms(planes, tile_x, tile_y)
    n_waves = matrices[0].shape[0]
    tile = min(256, channels)
    n_tiles = channels // tile
    edge = HALO * tile_x * tile_y
    n_half = n_row // 2
    parts = 2 if n_col <= 4 else 1
    outs = pl.pallas_call(
        functools.partial(block_kernel, (planes, tile_x, tile_y, n_dp, n_row, n_col)),
        out_shape=(
            jax.ShapeDtypeStruct((voxels, local), bf16),
            jax.ShapeDtypeStruct((voxels, local), bf16),
            jax.ShapeDtypeStruct((share, channels), bf16),
            jax.ShapeDtypeStruct((share, channels), bf16),
            jax.ShapeDtypeStruct((taps, channels), f32),
        ),
        in_specs=[anywhere] * 10,
        out_specs=(vmem,) * 5,
        scratch_shapes=[
            pltpu.VMEM(kernel.shape, f32),
            pltpu.VMEM((voxels, width), bf16),
            pltpu.VMEM((voxels, width), bf16),
            pltpu.VMEM((width, channels), bf16),
            pltpu.VMEM((width, channels), bf16),
            pltpu.VMEM((voxels, channels), bf16),
            pltpu.VMEM((voxels, channels), bf16),
            pltpu.VMEM((2 * edge, channels), bf16),
            pltpu.VMEM((2 * edge, channels), bf16),
            pltpu.VMEM((voxels, channels), f32),
            pltpu.VMEM((2, voxels, channels), bf16),
            pltpu.VMEM((2, voxels, channels), bf16),
            *(pltpu.VMEM(m.shape, bf16) for m in matrices),
            pltpu.VMEM((n_waves, channels), f32),
            pltpu.VMEM((n_waves, channels), f32),
            pltpu.VMEM((n_waves, channels), f32),
            pltpu.VMEM((2, 2, n_col, voxels, local), bf16),
            pltpu.VMEM((2, 2, n_col, voxels, local), bf16),
            pltpu.VMEM((2, voxels, local), f32),
            pltpu.VMEM((2, width, voxels), bf16),
            pltpu.VMEM((2, n_dp * n_half, share, voxels), bf16),
            pltpu.VMEM((2, n_half, share, channels), bf16),
            pltpu.VMEM((2, n_half, share, channels), bf16),
            pltpu.VMEM((2, n_half, share, channels), bf16),
            pltpu.VMEM((2, n_half, share, channels), bf16),
            pltpu.VMEM((tap_rows, channels), bf16),
            pltpu.VMEM((tap_rows, channels), bf16),
            pltpu.VMEM((tap_rows, channels // 2), bf16),
            pltpu.VMEM((n_row, tap_rows, channels // 2), bf16),
            pltpu.VMEM((tap_rows, channels // 2), f32),
            pltpu.VMEM((tap_rows, channels // 2), f32),
            dma((10,)),
            dma((2, n_col, parts)), dma((2, n_col, parts)),
            dma((n_col,)), dma((n_col,)),
            dma((2, 2, n_tiles)), dma((2, 2, n_tiles)),
            dma((2, 2, n_col, parts)), dma((2, 2, n_col, parts)),
            dma((2, n_dp * n_half)), dma((2, n_dp * n_half)),
            dma((2, n_tiles)), dma((2, n_tiles)),
            dma((2, n_half, n_tiles)), dma((2, n_half, n_tiles)),
            dma((2, n_half, n_tiles)), dma((2, n_half, n_tiles)),
            dma((n_row + 1,)), dma((n_row + 1,)),
        ],
        compiler_params=pltpu.CompilerParams(
            collective_id=0, has_side_effects=True, vmem_limit_bytes=60 << 20
        ),
    )(inputs.reshape(voxels, local), cotangent.reshape(voxels, local), up_weight, down_weight, kernel,
      *map(jnp.asarray, matrices))
    outs = pl.pallas_call(
        hand_on,
        out_shape=tuple(jax.ShapeDtypeStruct(out.shape, out.dtype) for out in outs),
        in_specs=[anywhere] * 5,
        out_specs=(anywhere,) * 5,
        scratch_shapes=[pltpu.VMEM(out.shape, out.dtype) for out in outs] + [dma((5,)), dma((5,))],
    )(*outs)
    return (outs[0].reshape(inputs.shape), outs[1].reshape(inputs.shape)) + tuple(outs[2:])


def solution(mesh):
    placed = (
        P("dp", "row", None, None, "col"),
        P(None, "col"),
        P(None, "col"),
        P(None, "col"),
        P("dp", "row", None, None, "col"),
    )
    return jax.shard_map(
        on_device,
        mesh=mesh,
        in_specs=placed,
        out_specs=(
            P("dp", "row", None, None, "col"),
            P("dp", "row", None, None, "col"),
            P(("dp", "row"), "col"),
            P(("dp", "row"), "col"),
            P(None, "col"),
        ),
        check_vma=False,
    )
```

```python
import functools

import jax
import jax.numpy as jnp
import ml_dtypes
import numpy as np
from jax import lax
from jax.experimental import pallas as pl
from jax.experimental.pallas import tpu as pltpu
from jax.sharding import PartitionSpec as P

HALO = 2


def aligned(index, size):
    return pl.ds(pl.multiple_of(index * size, size), size)


def transforms(planes, tile_x, tile_y, tap_rows):
    lengths = np.array([planes + 2 * HALO, tile_x + HALO, tile_y + HALO])
    waves = np.stack([m.ravel() for m in np.meshgrid(*map(np.arange, lengths), indexing="ij")], 1)
    mirrored = (-waves) % lengths
    code = waves @ np.array([lengths[1] * lengths[2], lengths[2], 1])
    mirrored_code = mirrored @ np.array([lengths[1] * lengths[2], lengths[2], 1])
    kept = code <= mirrored_code
    waves, weight = waves[kept], np.where(code == mirrored_code, 1.0, 2.0)[kept] / lengths.prod()
    rows = -(-len(waves) // 16) * 16

    def wave_matrix(*ranges):
        points = np.stack([m.ravel() for m in np.meshgrid(*ranges, indexing="ij")], 1)
        angle = 2 * np.pi * (waves / lengths) @ points.T
        both = np.zeros((2, rows, len(points)))
        both[0, : len(waves)], both[1, : len(waves)] = np.cos(angle), -np.sin(angle)
        return both

    weights = np.zeros(rows)
    weights[: len(waves)] = weight

    def forward(both):
        return both.reshape(2 * rows, -1)

    def backward(both):
        return (both * weights[:, None]).reshape(2 * rows, -1).T

    depth, along_x, along_y = np.arange(planes + 2 * HALO), np.arange(tile_x), np.arange(tile_y)
    reach = np.arange(-HALO, HALO + 1)
    grid = wave_matrix(depth, along_x, along_y)
    own = wave_matrix(depth[HALO:-HALO], along_x, along_y)
    taps = wave_matrix(reach, reach, reach)
    bf16 = ml_dtypes.bfloat16
    taps_high = forward(taps).astype(bf16)
    taps_low = (forward(taps) - taps_high.astype(np.float64)).astype(bf16)
    taps_back = backward(taps)
    taps_back = np.concatenate([taps_back, np.zeros((tap_rows - len(taps_back), taps_back.shape[1]))])
    edge = HALO * tile_x * tile_y
    to_waves = forward(grid)
    return tuple(
        m.astype(bf16)
        for m in (
            to_waves[:, edge:-edge], np.concatenate([to_waves[:, :edge], to_waves[:, -edge:]], 1),
            backward(own), np.stack([taps_high, taps_low]), taps_back,
        )
    )


def block_kernel(
    sizes, inputs, cotangent, up_weight, down_weight, stencil_weights,
    own_to_waves, halo_to_waves, from_waves, taps_to_waves, taps_from_waves,
    block_output, input_grad, up_grad, down_grad, kernel_grad,
    kernel, xg, cg, upw, dnw, hid, grd, hid_halo, grd_halo, wide, right, right_in,
    fwd_own, fwd_halo, inv, fwd_taps, inv_taps, tap_waves, hid_waves, grd_waves,
    sent, got, relay, own_sum, turned, turned_in, first_out, first_in, second_out, second_in,
    taps_out, taps_in, share_out, share_in, half_out, half_in,
    load_sem, ag_s, ag_r, cot_s, cot_r, halo_s, halo_r, sum_out_s, sum_out_r, relay_r, piece_s, piece_r,
    gather_s, gather_r, pair_s, pair_r, row_s, row_r, kg_s, kg_r, sum_s, sum_r,
):
    planes, tile_x, tile_y, n_dp, n_row, n_col = sizes
    dp, row, col = lax.axis_index("dp"), lax.axis_index("row"), lax.axis_index("col")
    partner = {"dp": 1 - dp}
    voxels, local = inputs.shape
    channels = kernel.shape[1]
    edge = HALO * tile_x * tile_y
    tile = min(256, channels)
    n_tiles = channels // tile
    wtile = min(256, local)
    parts = ag_s.shape[2]
    part_rows = voxels // parts
    n_half = n_row // 2
    share = first_out.shape[2]
    bf16, f32 = jnp.bfloat16, jnp.float32
    mine = aligned(col, local)
    act, hgr = right.at[0], right.at[1]

    loads = [
        pltpu.make_async_copy(source, target, load_sem.at[i])
        for i, (source, target) in enumerate((
            (inputs, xg.at[:, mine]), (up_weight, upw), (stencil_weights, kernel), (cotangent, cg.at[:, mine]),
            (down_weight, dnw), (own_to_waves, fwd_own), (halo_to_waves, fwd_halo), (from_waves, inv),
            (taps_to_waves, fwd_taps), (taps_from_waves, inv_taps),
        ))
    ]
    for i in (0, 2, 8, 1, 5, 6, 7, 3, 4, 9):
        loads[i].start()

    barrier = pltpu.get_barrier_semaphore()

    for side in (1, -1):
        @pl.when(jnp.logical_and(col + side >= 0, col + side < n_col))
        def _():
            pl.semaphore_signal(barrier, inc=1, device_id={"col": col + side})

    @pl.loop(1, n_row)
    def _(k):
        pl.semaphore_signal(barrier, inc=1, device_id={"row": lax.rem(row + k, n_row)})

    pl.semaphore_signal(barrier, inc=1, device_id=partner)
    ends = jnp.where(col == 0, 1, 0) + jnp.where(col == n_col - 1, 1, 0)
    pl.semaphore_wait(barrier, n_row + 2 - ends)

    def remote(source, target, send, receive, device):
        return pltpu.make_async_remote_copy(
            src_ref=source, dst_ref=target, send_sem=send, recv_sem=receive,
            device_id=device, device_id_type=pl.DeviceIdType.MESH,
        )

    def each(count, action, first=0):
        @pl.loop(first, count)
        def _(k):
            action(k)

    def inside(index):
        return jnp.logical_and(index >= 0, index < n_col)

    def hop(side, step, part):
        rows = slice(part * part_rows, (part + 1) * part_rows)
        place = xg.at[rows, aligned(col - side * step, local)]
        return remote(
            inputs.at[rows] if step == 0 else place, place,
            ag_s.at[(side + 1) // 2, step, part], ag_r.at[(side + 1) // 2, step, part], {"col": col + side},
        )

    def hop_goes(side, step):
        return jnp.logical_and(inside(col + side), inside(col - side * step))

    def hop_start(step, part):
        for side in (1, -1):
            pl.when(hop_goes(side, step))(hop(side, step, part).start)

    def hop_received(step, part):
        for side in (1, -1):
            pl.when(inside(col - side * (step + 1)))(hop(side, step, part).wait_recv)

    def cot_copy(peer, source):
        return remote(cotangent, cg.at[:, aligned(source, local)], cot_s.at[peer], cot_r.at[source], {"col": peer})

    def cot_start(slot):
        pl.when(slot > col)(lambda: cot_copy(slot, col).start())
        pl.when(n_col - 1 - slot < col)(lambda: cot_copy(n_col - 1 - slot, col).start())

    def side_of(i, r):
        return r // n_half if i == 0 else lax.rem(r, 2)

    def place_of(i, r):
        return lax.rem(r, n_half) if i == 0 else r // 2

    def row_of(i, side, place):
        return side * n_half + place if i == 0 else 2 * place + side

    def mate(i):
        return {"row": row_of(i, 1 - side_of(i, row), place_of(i, row))}

    def piece(i, index):
        slot = (index // n_row) * n_half + place_of(i, lax.rem(index, n_row))
        return remote(
            turned.at[i, aligned(index, share)], turned_in.at[i, slot], piece_s.at[i, slot], piece_r.at[i, slot], mate(i)
        )

    def leaves(i, index):
        return side_of(i, lax.rem(index, n_row)) != side_of(i, row)

    def turn(i, field, shard):
        turned[i, aligned(shard, local)] = field[:, aligned(shard, local)].T
        for k in range(local // share):
            index = shard * (local // share) + k
            pl.when(leaves(i, index))(lambda: piece(i, index).start())

    for part in range(parts):
        hop_start(0, part)

    def zero_edges(side):
        for halo in (hid_halo, grd_halo):
            halo[side * edge : (side + 1) * edge] = jnp.zeros((edge, channels), bf16)

    pl.when(row == 0)(lambda: zero_edges(0))
    pl.when(row == n_row - 1)(lambda: zero_edges(1))
    loads[2].wait()
    loads[8].wait()

    @pl.loop(0, n_tiles)
    def _(n):
        cols = aligned(n, tile)
        weights = kernel[:, cols]
        high = weights.astype(bf16)
        low = (weights - high.astype(f32)).astype(bf16)
        tap_waves[:, cols] = (
            jnp.dot(fwd_taps[0], high, preferred_element_type=f32)
            + jnp.dot(fwd_taps[1], high, preferred_element_type=f32)
            + jnp.dot(fwd_taps[0], low, preferred_element_type=f32)
        )

    loads[0].wait()
    loads[1].wait()

    def expand(shard, cols):
        return jnp.dot(xg[:, aligned(shard, local)], upw[aligned(shard, local), cols], preferred_element_type=f32)

    @pl.loop(0, n_tiles)
    def _(n):
        cols = aligned(n, tile)
        wide[:, cols] = expand(col, cols)

    turn(1, xg, col)
    loads[3].wait()
    turn(0, cg, col)
    for slot in range(1, n_col - 1):
        for part in range(parts):
            hop_received(slot - 1, part)
            hop_start(slot, part)
        cot_start(slot)
        for side in (1, -1):
            shard = col - side * slot

            @pl.when(inside(shard))
            def _():
                @pl.loop(0, n_tiles)
                def _(n):
                    cols = aligned(n, tile)
                    wide[:, cols] = wide[:, cols] + expand(shard, cols)

                turn(1, xg, shard)

    last = n_col - 1 - col
    at_end = jnp.logical_or(col == 0, last == 0)

    def halo(i, field, edges, side, cols, n):
        if side:
            source, target, peer = 0, edge, row - 1
        else:
            source, target, peer = voxels - edge, 0, row + 1
        return remote(
            field.at[source : source + edge, cols], edges.at[target : target + edge, cols],
            halo_s.at[i, side, n], halo_r.at[i, side, n], {"row": peer},
        )

    def halo_start(i, field, edges, side, cols, n):
        pl.when(row > 0 if side else row < n_row - 1)(lambda: halo(i, field, edges, side, cols, n).start())

    def halo_received(i, field, edges, cols, n):
        pl.when(row > 0)(lambda: halo(i, field, edges, 0, cols, n).wait_recv())
        pl.when(row < n_row - 1)(lambda: halo(i, field, edges, 1, cols, n).wait_recv())

    def halo_sent(i, field, edges, cols, n):
        pl.when(row < n_row - 1)(lambda: halo(i, field, edges, 0, cols, n).wait_send())
        pl.when(row > 0)(lambda: halo(i, field, edges, 1, cols, n).wait_send())

    def gather(i, cols, n):
        return remote(
            right.at[i, :, cols], right_in.at[i, :, cols], gather_s.at[i, n], gather_r.at[i, n], mate(i)
        )

    for part in range(parts):
        hop_received(n_col - 2, part)
        if part == 0:
            cot_start(n_col - 1)
        rows = slice(part * part_rows, (part + 1) * part_rows)

        @pl.loop(0, n_tiles)
        def _(n):
            cols = aligned(n, tile)

            @pl.when(at_end)
            def _():
                wide[rows, cols] = wide[rows, cols] + jnp.dot(
                    xg[rows, aligned(last, local)], upw[aligned(last, local), cols], preferred_element_type=f32
                )

            hid[rows, cols] = wide[rows, cols].astype(bf16)
            for side, ready in ((1, part == (edge - 1) // part_rows), (0, part == parts - 1)):
                if ready:
                    halo_start(0, hid, hid_halo, side, cols, n)

    for i in (5, 6, 7):
        loads[i].wait()

    def waves_of(matrix, field, cols):
        return jnp.dot(matrix[...], field[:, cols], preferred_element_type=f32)

    def own_waves(waves, field, cols):
        waves[:, cols] = waves_of(fwd_own, field, cols)

    each(n_tiles, lambda n: own_waves(hid_waves, hid, aligned(n, tile)))

    half_waves = tap_waves.shape[0] // 2

    def product(left, other, cols, conjugate):
        lr, li = left[0:half_waves, cols], left[half_waves : 2 * half_waves, cols]
        rr, ri = other[0:half_waves, cols], other[half_waves : 2 * half_waves, cols]
        if conjugate:
            return jnp.concatenate([(lr * rr + li * ri).astype(bf16), (li * rr - lr * ri).astype(bf16)])
        return jnp.concatenate([(lr * rr - li * ri).astype(bf16), (li * rr + lr * ri).astype(bf16)])

    @pl.loop(0, n_tiles)
    def _(n):
        cols = aligned(n, tile)
        halo_received(0, hid, hid_halo, cols, n)
        hid_waves[:, cols] = hid_waves[:, cols] + waves_of(fwd_halo, hid_halo, cols)
        preact = jnp.dot(inv[...], product(hid_waves, tap_waves, cols, True), preferred_element_type=f32)
        wide[:, cols] = preact
        act[:, cols] = (preact * jax.nn.sigmoid(preact)).astype(bf16)
        gather(0, cols, n).start()

    pl.when(at_end)(lambda: turn(1, xg, last))

    def project(left, weight, dest, out):
        @pl.loop(0, local // wtile)
        def _(n):
            rows = pl.ds(pl.multiple_of(dest * local + n * wtile, wtile), wtile)
            out[:, aligned(n, wtile)] = lax.dot_general(
                left[...], weight[rows, :], (((1,), (1,)), ((), ())), preferred_element_type=f32
            ).astype(out.dtype)

    def partial(i, dest, source, part):
        rows = slice(part * part_rows, (part + 1) * part_rows)
        return remote(
            sent.at[i, dest, rows], got.at[i, source, rows], sum_out_s.at[i, dest, part], sum_out_r.at[i, source, part],
            {"col": dest},
        )

    def passed(i, side, part):
        rows = slice(part * part_rows, (part + 1) * part_rows)
        return remote(
            sent.at[i, 0 if side else n_col - 1, rows], relay.at[i, side, rows],
            sum_out_s.at[i, 0 if side else n_col - 1, part], relay_r.at[i, side, part],
            {"col": n_col - 2 if side else 1},
        )

    def targets(m):
        far = n_col - 1 - m
        return (
            (0, far, far > col, jnp.logical_and(far == n_col - 1, col == 0), jnp.logical_and(far == n_col - 1, col == 1)),
            (1, m, m < col, jnp.logical_and(m == 0, last == 0), jnp.logical_and(m == 0, last == 1)),
        )

    def sums_begin(i, left, weight):
        @pl.loop(0, n_col - 1)
        def _(m):
            for side, dest, goes, ends, joins in targets(m):
                @pl.when(goes)
                def _():
                    project(left, weight, dest, sent.at[i, dest])
                    for part in range(parts):
                        pl.when(ends)(lambda: passed(i, side, part).start())
                        pl.when(jnp.logical_not(jnp.logical_or(ends, joins)))(lambda: partial(i, dest, col, part).start())

    def sums_join(i):
        for part in range(parts):
            rows = slice(part * part_rows, (part + 1) * part_rows)
            for side, dest, joins in ((0, n_col - 1, col == 1), (1, 0, last == 1)):
                @pl.when(joins)
                def _():
                    passed(i, side, part).wait_recv()
                    total = sent[i, dest, rows].astype(f32) + relay[i, side, rows].astype(f32)
                    sent[i, dest, rows] = total.astype(bf16)
                    partial(i, dest, col, part).start()

    def sums_end(i, residual, out):
        @pl.loop(0, n_col)
        def _(k):
            ends = jnp.logical_or(jnp.logical_and(k == 0, last == 0), jnp.logical_and(k == n_col - 1, col == 0))

            @pl.when(jnp.logical_and(k != col, jnp.logical_not(ends)))
            def _():
                for part in range(parts):
                    partial(i, col, k, part).wait_recv()
                own_sum[i] = own_sum[i] + got[i, k].astype(f32)

        out[...] = (residual[:, mine].astype(f32) + own_sum[i]).astype(bf16)

    def sums_sent(i):
        @pl.loop(0, n_col)
        def _(k):
            @pl.when(k != col)
            def _():
                for part in range(parts):
                    partial(i, k, col, part).wait_send()

    loads[4].wait()
    sums_begin(0, act, dnw)

    @pl.loop(0, n_col)
    def _(k):
        pl.when(k != col)(lambda: cot_copy(col, k).wait_recv())

    @pl.loop(0, n_tiles)
    def _(n):
        cols = aligned(n, tile)
        act_grad = jnp.dot(cg[...], dnw[:, cols], preferred_element_type=f32)
        preact = wide[:, cols]
        logistic = jax.nn.sigmoid(preact)
        grd[:, cols] = (act_grad * logistic * (1.0 + preact * (1.0 - logistic))).astype(bf16)
        halo_start(1, grd, grd_halo, 1, cols, n)
        halo_start(1, grd, grd_halo, 0, cols, n)

    each(n_col, lambda k: pl.when(k != col)(lambda: turn(0, cg, k)))
    each(n_tiles, lambda n: own_waves(grd_waves, grd, aligned(n, tile)))
    loads[9].wait()

    @pl.loop(0, n_tiles)
    def _(n):
        cols = aligned(n, tile)
        taps_out[:, cols] = jnp.dot(
            inv_taps[...], product(hid_waves, grd_waves, cols, True), preferred_element_type=f32
        ).astype(bf16)

    some, others = aligned(dp, channels // 2), aligned(1 - dp, channels // 2)
    whole_taps = remote(taps_out.at[:, others], taps_in, kg_s.at[0], kg_r.at[0], partner)
    whole_taps.start()
    project(act, dnw, col, own_sum.at[0])
    sums_join(0)

    @pl.loop(0, n_tiles)
    def _(n):
        cols = aligned(n, tile)
        halo_received(1, grd, grd_halo, cols, n)
        grd_waves[:, cols] = grd_waves[:, cols] + waves_of(fwd_halo, grd_halo, cols)
        hgr[:, cols] = jnp.dot(
            inv[...], product(grd_waves, tap_waves, cols, False), preferred_element_type=f32
        ).astype(bf16)
        gather(1, cols, n).start()

    sums_begin(1, hgr, upw)

    def pair(i, j, cols, n):
        return remote(first_out.at[i, j, :, cols], first_in.at[i, j, :, cols], pair_s.at[i, j, n], pair_r.at[i, j, n], partner)

    def row_copy(i, to, source, cols, n):
        return remote(
            second_out.at[i, to, :, cols], second_in.at[i, source, :, cols], row_s.at[i, to, n], row_r.at[i, source, n],
            {"row": row_of(i, side_of(i, row), to)},
        )

    def outer(i, half, j, cols):
        index = half * n_row + row_of(i, side_of(i, row), j)
        return jnp.dot(
            turned[i, aligned(index, share)], right[i, :, cols], preferred_element_type=f32
        ) + jnp.dot(turned_in[i, half * n_half + j], right_in[i, :, cols], preferred_element_type=f32)

    def grad_for_partner(i, n):
        cols = aligned(n, tile)
        gather(i, cols, n).wait_recv()

        @pl.loop(0, n_half)
        def _(j):
            first_out[i, j, :, cols] = outer(i, 1 - dp, j, cols).astype(bf16)
            pair(i, j, cols, n).start()

    def grad_own(i, n):
        cols = aligned(n, tile)
        here = place_of(i, row)

        @pl.loop(0, n_half)
        def _(j):
            total = outer(i, dp, j, cols)
            pair(i, j, cols, n).wait_recv()
            second_out[i, j, :, cols] = (total + first_in[i, j, :, cols].astype(f32)).astype(bf16)
            if i:
                pl.when(j != here)(lambda: row_copy(i, j, here, cols, n).start())

    def rows_start(i, n):
        here = place_of(i, row)
        each(n_half, lambda j: pl.when(j != here)(lambda: row_copy(i, j, here, aligned(n, tile), n).start()))

    def grad_step(i, step):
        pl.when(step < n_tiles)(lambda: grad_for_partner(i, step))
        pl.when(jnp.logical_and(step > 0, step <= n_tiles))(lambda: grad_own(i, step - 1))

    def grad_finish(i, out):
        here = place_of(i, row)

        @pl.loop(0, n_tiles)
        def _(n):
            cols = aligned(n, tile)
            own_sum_tile = second_out[i, here, :, cols].astype(f32)
            for k in range(1, n_half):
                source = lax.rem(here + k, n_half)
                row_copy(i, here, source, cols, n).wait_recv()
                own_sum_tile = own_sum_tile + second_in[i, source, :, cols].astype(f32)
            out[:, cols] = own_sum_tile.astype(bf16)

    def pieces_received(i):
        @pl.loop(0, n_dp * n_half)
        def _(slot):
            index = (slot // n_half) * n_row + row_of(i, 1 - side_of(i, row), lax.rem(slot, n_half))
            piece(i, index).wait_recv()

    pieces_received(0)
    each(n_tiles + 1, lambda step: grad_step(0, step))
    whole_taps.wait_recv()
    share_out[...] = (taps_out[:, some].astype(f32) + taps_in[...].astype(f32)).astype(bf16)
    tap_share = share_out.shape[0] // n_row

    def taps_copy(k):
        peer = lax.rem(row + k, n_row)
        return remote(share_out.at[aligned(peer, tap_share)], share_in.at[k], kg_s.at[k], kg_r.at[k], {"row": peer})

    def taps_sum(k, source):
        target = half_out.at[aligned(source, tap_share)]
        return remote(
            half_out.at[aligned(row, tap_share)], target, sum_s.at[k], sum_r.at[k], {"row": lax.rem(row + k, n_row)}
        )

    each(n_row, lambda k: taps_copy(k).start(), 1)
    sums_end(0, xg, block_output)
    sums_join(1)
    project(hgr, upw, col, own_sum.at[1])
    pieces_received(1)

    @pl.loop(0, n_tiles + 1)
    def _(step):
        grad_step(1, step)
        pl.when(step < n_tiles)(lambda: rows_start(0, step))

    each(n_row, lambda k: taps_copy(k).wait_recv(), 1)
    my_taps = aligned(row, tap_share)
    total = share_out[my_taps].astype(f32)
    for k in range(1, n_row):
        total = total + share_in[k].astype(f32)
    half_out[my_taps] = total.astype(bf16)
    each(n_row, lambda k: taps_sum(k, row).start(), 1)
    grad_finish(0, down_grad)
    each(n_row, lambda k: taps_sum(k, lax.rem(row + n_row - k, n_row)).wait_recv(), 1)
    halves = remote(half_out, half_in, kg_s.at[n_row], kg_r.at[n_row], partner)
    halves.start()
    n_taps = kernel.shape[0]
    kernel_grad[:, some] = half_out[...].astype(f32)[0:n_taps]
    grad_finish(1, up_grad)
    sums_end(1, cg, input_grad)
    halves.wait_recv()
    kernel_grad[:, others] = half_in[...].astype(f32)[0:n_taps]

    for step in range(n_col - 1):
        for part in range(parts):
            for side in (1, -1):
                pl.when(hop_goes(side, step))(hop(side, step, part).wait_send)
    each(n_col, lambda k: pl.when(k != col)(lambda: cot_copy(k, col).wait_send()))
    for i in range(2):
        sums_sent(i)
        each(n_dp * n_row, lambda k: pl.when(leaves(i, k))(lambda: piece(i, k).wait_send()))

        @pl.loop(0, n_tiles)
        def _(n):
            cols = aligned(n, tile)
            halo_sent(i, (hid, grd)[i], (hid_halo, grd_halo)[i], cols, n)
            gather(i, cols, n).wait_send()
            here = place_of(i, row)
            for j in range(n_half):
                pair(i, j, cols, n).wait_send()
                pl.when(j != here)(lambda: row_copy(i, j, here, cols, n).wait_send())

    whole_taps.wait_send()
    each(n_row, lambda k: taps_copy(k).wait_send(), 1)
    each(n_row, lambda k: taps_sum(k, row).wait_send(), 1)
    halves.wait_send()


def hand_on(*refs):
    arrived, done = refs[15], refs[16]
    fetches = [pltpu.make_async_copy(refs[i], refs[10 + i], arrived.at[i]) for i in range(5)]
    stores = [pltpu.make_async_copy(refs[10 + i], refs[5 + i], done.at[i]) for i in range(5)]
    for fetch in fetches:
        fetch.start()
    for fetch, store in zip(fetches, stores):
        fetch.wait()
        store.start()
    for store in stores:
        store.wait()


def on_device(inputs, up_weight, down_weight, kernel, cotangent):
    _, planes, tile_x, tile_y, local = inputs.shape
    n_dp, n_row, n_col = (lax.axis_size(name) for name in ("dp", "row", "col"))
    voxels = planes * tile_x * tile_y
    extended = voxels + 2 * HALO * tile_x * tile_y
    width, channels = up_weight.shape
    share = width // (n_dp * n_row)
    bf16, f32 = jnp.bfloat16, jnp.float32
    dma = pltpu.SemaphoreType.DMA
    taps = kernel.shape[0]
    tap_rows = -(-taps // (16 * n_row)) * 16 * n_row
    vmem, anywhere = pl.BlockSpec(memory_space=pltpu.VMEM), pl.BlockSpec(memory_space=pl.ANY)
    matrices = transforms(planes, tile_x, tile_y, tap_rows)
    n_waves = matrices[0].shape[0]
    tile = min(256, channels)
    n_tiles = channels // tile
    edge = HALO * tile_x * tile_y
    n_half = n_row // 2
    parts = 2 if n_col <= 4 else 1
    outs = pl.pallas_call(
        functools.partial(block_kernel, (planes, tile_x, tile_y, n_dp, n_row, n_col)),
        out_shape=(
            jax.ShapeDtypeStruct((voxels, local), bf16),
            jax.ShapeDtypeStruct((voxels, local), bf16),
            jax.ShapeDtypeStruct((share, channels), bf16),
            jax.ShapeDtypeStruct((share, channels), bf16),
            jax.ShapeDtypeStruct((taps, channels), f32),
        ),
        in_specs=[anywhere] * 10,
        out_specs=(vmem,) * 5,
        scratch_shapes=[
            pltpu.VMEM(kernel.shape, f32),
            pltpu.VMEM((voxels, width), bf16),
            pltpu.VMEM((voxels, width), bf16),
            pltpu.VMEM((width, channels), bf16),
            pltpu.VMEM((width, channels), bf16),
            pltpu.VMEM((voxels, channels), bf16),
            pltpu.VMEM((voxels, channels), bf16),
            pltpu.VMEM((2 * edge, channels), bf16),
            pltpu.VMEM((2 * edge, channels), bf16),
            pltpu.VMEM((voxels, channels), f32),
            pltpu.VMEM((2, voxels, channels), bf16),
            pltpu.VMEM((2, voxels, channels), bf16),
            *(pltpu.VMEM(m.shape, bf16) for m in matrices),
            pltpu.VMEM((n_waves, channels), f32),
            pltpu.VMEM((n_waves, channels), f32),
            pltpu.VMEM((n_waves, channels), f32),
            pltpu.VMEM((2, n_col, voxels, local), bf16),
            pltpu.VMEM((2, n_col, voxels, local), bf16),
            pltpu.VMEM((2, 2, voxels, local), bf16),
            pltpu.VMEM((2, voxels, local), f32),
            pltpu.VMEM((2, width, voxels), bf16),
            pltpu.VMEM((2, n_dp * n_half, share, voxels), bf16),
            pltpu.VMEM((2, n_half, share, channels), bf16),
            pltpu.VMEM((2, n_half, share, channels), bf16),
            pltpu.VMEM((2, n_half, share, channels), bf16),
            pltpu.VMEM((2, n_half, share, channels), bf16),
            pltpu.VMEM((tap_rows, channels), bf16),
            pltpu.VMEM((tap_rows, channels // 2), bf16),
            pltpu.VMEM((tap_rows, channels // 2), bf16),
            pltpu.VMEM((n_row, tap_rows // n_row, channels // 2), bf16),
            pltpu.VMEM((tap_rows, channels // 2), bf16),
            pltpu.VMEM((tap_rows, channels // 2), bf16),
            dma((10,)),
            dma((2, n_col, parts)), dma((2, n_col, parts)),
            dma((n_col,)), dma((n_col,)),
            dma((2, 2, n_tiles)), dma((2, 2, n_tiles)),
            dma((2, n_col, parts)), dma((2, n_col, parts)), dma((2, 2, parts)),
            dma((2, n_dp * n_half)), dma((2, n_dp * n_half)),
            dma((2, n_tiles)), dma((2, n_tiles)),
            dma((2, n_half, n_tiles)), dma((2, n_half, n_tiles)),
            dma((2, n_half, n_tiles)), dma((2, n_half, n_tiles)),
            dma((n_row + 1,)), dma((n_row + 1,)),
            dma((n_row,)), dma((n_row,)),
        ],
        compiler_params=pltpu.CompilerParams(
            collective_id=0, has_side_effects=True, vmem_limit_bytes=60 << 20
        ),
    )(inputs.reshape(voxels, local), cotangent.reshape(voxels, local), up_weight, down_weight, kernel,
      *map(jnp.asarray, matrices))
    outs = pl.pallas_call(
        hand_on,
        out_shape=tuple(jax.ShapeDtypeStruct(out.shape, out.dtype) for out in outs),
        in_specs=[anywhere] * 5,
        out_specs=(anywhere,) * 5,
        scratch_shapes=[pltpu.VMEM(out.shape, out.dtype) for out in outs] + [dma((5,)), dma((5,))],
    )(*outs)
    return (outs[0].reshape(inputs.shape), outs[1].reshape(inputs.shape)) + tuple(outs[2:])


def solution(mesh):
    placed = (
        P("dp", "row", None, None, "col"),
        P(None, "col"),
        P(None, "col"),
        P(None, "col"),
        P("dp", "row", None, None, "col"),
    )
    return jax.shard_map(
        on_device,
        mesh=mesh,
        in_specs=placed,
        out_specs=(
            P("dp", "row", None, None, "col"),
            P("dp", "row", None, None, "col"),
            P(("dp", "row"), "col"),
            P(("dp", "row"), "col"),
            P(None, "col"),
        ),
        check_vma=False,
    )
```

```python
import functools

import jax
import jax.numpy as jnp
import ml_dtypes
import numpy as np
from jax import lax
from jax.experimental import pallas as pl
from jax.experimental.pallas import tpu as pltpu
from jax.sharding import PartitionSpec as P

HALO = 2


def aligned(index, size):
    return pl.ds(pl.multiple_of(index * size, size), size)


def transforms(planes, tile_x, tile_y, tap_rows):
    lengths = np.array([planes + 2 * HALO, tile_x + HALO, tile_y + HALO])
    waves = np.stack([m.ravel() for m in np.meshgrid(*map(np.arange, lengths), indexing="ij")], 1)
    mirrored = (-waves) % lengths
    code = waves @ np.array([lengths[1] * lengths[2], lengths[2], 1])
    mirrored_code = mirrored @ np.array([lengths[1] * lengths[2], lengths[2], 1])
    kept = code <= mirrored_code
    waves, weight = waves[kept], np.where(code == mirrored_code, 1.0, 2.0)[kept] / lengths.prod()
    rows = -(-len(waves) // 16) * 16

    def wave_matrix(*ranges):
        points = np.stack([m.ravel() for m in np.meshgrid(*ranges, indexing="ij")], 1)
        angle = 2 * np.pi * (waves / lengths) @ points.T
        both = np.zeros((2, rows, len(points)))
        both[0, : len(waves)], both[1, : len(waves)] = np.cos(angle), -np.sin(angle)
        return both

    weights = np.zeros(rows)
    weights[: len(waves)] = weight

    def forward(both):
        return both.reshape(2 * rows, -1)

    def backward(both):
        return (both * weights[:, None]).reshape(2 * rows, -1).T

    depth, along_x, along_y = np.arange(planes + 2 * HALO), np.arange(tile_x), np.arange(tile_y)
    reach = np.arange(-HALO, HALO + 1)
    grid = wave_matrix(depth, along_x, along_y)
    own = wave_matrix(depth[HALO:-HALO], along_x, along_y)
    taps = wave_matrix(reach, reach, reach)
    bf16 = ml_dtypes.bfloat16
    taps_high = forward(taps).astype(bf16)
    taps_low = (forward(taps) - taps_high.astype(np.float64)).astype(bf16)
    taps_back = backward(taps)
    taps_back = np.concatenate([taps_back, np.zeros((tap_rows - len(taps_back), taps_back.shape[1]))])
    edge = HALO * tile_x * tile_y
    to_waves = forward(grid)
    return tuple(
        m.astype(bf16)
        for m in (
            to_waves[:, edge:-edge], np.concatenate([to_waves[:, :edge], to_waves[:, -edge:]], 1),
            backward(own), np.stack([taps_high, taps_low]), taps_back,
        )
    )


def block_kernel(
    sizes, inputs, cotangent, up_weight, down_weight, stencil_weights,
    own_to_waves, halo_to_waves, from_waves, taps_to_waves, taps_from_waves,
    block_output, input_grad, up_grad, down_grad, kernel_grad,
    kernel, xg, cg, upw, dnw, hid, grd, hid_halo, grd_halo, wide, right, right_in,
    fwd_own, fwd_halo, inv, fwd_taps, inv_taps, tap_waves, hid_waves, grd_waves,
    sent, got, relay, own_sum, turned, turned_in, first_out, first_in, second_out, second_in,
    taps_out, taps_in, share_out, share_in, half_out, half_in,
    load_sem, ag_s, ag_r, cot_s, cot_r, halo_s, halo_r, sum_out_s, sum_out_r, relay_r, piece_s, piece_r,
    gather_s, gather_r, pair_s, pair_r, row_s, row_r, kg_s, kg_r, sum_s, sum_r,
):
    planes, tile_x, tile_y, n_dp, n_row, n_col = sizes
    dp, row, col = lax.axis_index("dp"), lax.axis_index("row"), lax.axis_index("col")
    partner = {"dp": 1 - dp}
    voxels, local = inputs.shape
    channels = kernel.shape[1]
    edge = HALO * tile_x * tile_y
    tile = min(256, channels)
    n_tiles = channels // tile
    wtile = min(256, local)
    parts = ag_s.shape[2]
    part_rows = voxels // parts
    n_half = n_row // 2
    share = first_out.shape[2]
    bf16, f32 = jnp.bfloat16, jnp.float32
    mine = aligned(col, local)
    act, hgr = right.at[0], right.at[1]

    loads = [
        pltpu.make_async_copy(source, target, load_sem.at[i])
        for i, (source, target) in enumerate((
            (inputs, xg.at[:, mine]), (up_weight, upw), (stencil_weights, kernel), (cotangent, cg.at[:, mine]),
            (down_weight, dnw), (own_to_waves, fwd_own), (halo_to_waves, fwd_halo), (from_waves, inv),
            (taps_to_waves, fwd_taps), (taps_from_waves, inv_taps),
        ))
    ]
    for i in (0, 2, 8, 1, 5, 6, 7, 3, 4, 9):
        loads[i].start()

    barrier = pltpu.get_barrier_semaphore()

    for side in (1, -1):
        @pl.when(jnp.logical_and(col + side >= 0, col + side < n_col))
        def _():
            pl.semaphore_signal(barrier, inc=1, device_id={"col": col + side})

    @pl.loop(1, n_row)
    def _(k):
        pl.semaphore_signal(barrier, inc=1, device_id={"row": lax.rem(row + k, n_row)})

    pl.semaphore_signal(barrier, inc=1, device_id=partner)
    ends = jnp.where(col == 0, 1, 0) + jnp.where(col == n_col - 1, 1, 0)
    pl.semaphore_wait(barrier, n_row + 2 - ends)

    def remote(source, target, send, receive, device):
        return pltpu.make_async_remote_copy(
            src_ref=source, dst_ref=target, send_sem=send, recv_sem=receive,
            device_id=device, device_id_type=pl.DeviceIdType.MESH,
        )

    def each(count, action, first=0):
        @pl.loop(first, count)
        def _(k):
            action(k)

    def inside(index):
        return jnp.logical_and(index >= 0, index < n_col)

    def hop(side, step, part):
        rows = slice(part * part_rows, (part + 1) * part_rows)
        place = xg.at[rows, aligned(col - side * step, local)]
        return remote(
            inputs.at[rows] if step == 0 else place, place,
            ag_s.at[(side + 1) // 2, step, part], ag_r.at[(side + 1) // 2, step, part], {"col": col + side},
        )

    def hop_goes(side, step):
        return jnp.logical_and(inside(col + side), inside(col - side * step))

    def hop_start(step, part):
        for side in (1, -1):
            pl.when(hop_goes(side, step))(hop(side, step, part).start)

    def hop_received(step, part):
        for side in (1, -1):
            pl.when(inside(col - side * (step + 1)))(hop(side, step, part).wait_recv)

    def cot_copy(peer, source):
        return remote(cotangent, cg.at[:, aligned(source, local)], cot_s.at[peer], cot_r.at[source], {"col": peer})

    def cot_start(slot):
        pl.when(slot > col)(lambda: cot_copy(slot, col).start())
        pl.when(n_col - 1 - slot < col)(lambda: cot_copy(n_col - 1 - slot, col).start())

    def side_of(i, r):
        return r // n_half if i == 0 else lax.rem(r, 2)

    def place_of(i, r):
        return lax.rem(r, n_half) if i == 0 else r // 2

    def row_of(i, side, place):
        return side * n_half + place if i == 0 else 2 * place + side

    def mate(i):
        return {"row": row_of(i, 1 - side_of(i, row), place_of(i, row))}

    def piece(i, index):
        slot = (index // n_row) * n_half + place_of(i, lax.rem(index, n_row))
        return remote(
            turned.at[i, aligned(index, share)], turned_in.at[i, slot], piece_s.at[i, slot], piece_r.at[i, slot], mate(i)
        )

    def leaves(i, index):
        return side_of(i, lax.rem(index, n_row)) != side_of(i, row)

    def turn(i, field, shard):
        turned[i, aligned(shard, local)] = field[:, aligned(shard, local)].T
        for k in range(local // share):
            index = shard * (local // share) + k
            pl.when(leaves(i, index))(lambda: piece(i, index).start())

    hop_start(0, 0)

    def zero_edges(side):
        for halo in (hid_halo, grd_halo):
            halo[side * edge : (side + 1) * edge] = jnp.zeros((edge, channels), bf16)

    pl.when(row == 0)(lambda: zero_edges(0))
    pl.when(row == n_row - 1)(lambda: zero_edges(1))
    loads[2].wait()
    loads[8].wait()

    @pl.loop(0, n_tiles)
    def _(n):
        cols = aligned(n, tile)
        weights = kernel[:, cols]
        high = weights.astype(bf16)
        low = (weights - high.astype(f32)).astype(bf16)
        tap_waves[:, cols] = (
            jnp.dot(fwd_taps[0], high, preferred_element_type=f32)
            + jnp.dot(fwd_taps[1], high, preferred_element_type=f32)
            + jnp.dot(fwd_taps[0], low, preferred_element_type=f32)
        )

    for part in range(1, parts):
        hop_start(0, part)
    loads[0].wait()
    loads[1].wait()

    def expand(shard, cols):
        return jnp.dot(xg[:, aligned(shard, local)], upw[aligned(shard, local), cols], preferred_element_type=f32)

    @pl.loop(0, n_tiles)
    def _(n):
        cols = aligned(n, tile)
        wide[:, cols] = expand(col, cols)

    turn(1, xg, col)
    loads[3].wait()
    turn(0, cg, col)
    for slot in range(1, n_col - 1):
        for part in range(parts):
            hop_received(slot - 1, part)
            hop_start(slot, part)
        cot_start(slot)
        for side in (1, -1):
            shard = col - side * slot

            @pl.when(inside(shard))
            def _():
                @pl.loop(0, n_tiles)
                def _(n):
                    cols = aligned(n, tile)
                    wide[:, cols] = wide[:, cols] + expand(shard, cols)

                turn(1, xg, shard)

    last = n_col - 1 - col
    at_end = jnp.logical_or(col == 0, last == 0)

    def halo(i, field, edges, side, cols, n):
        if side:
            source, target, peer = 0, edge, row - 1
        else:
            source, target, peer = voxels - edge, 0, row + 1
        return remote(
            field.at[source : source + edge, cols], edges.at[target : target + edge, cols],
            halo_s.at[i, side, n], halo_r.at[i, side, n], {"row": peer},
        )

    def halo_start(i, field, edges, side, cols, n):
        pl.when(row > 0 if side else row < n_row - 1)(lambda: halo(i, field, edges, side, cols, n).start())

    def halo_received(i, field, edges, cols, n):
        pl.when(row > 0)(lambda: halo(i, field, edges, 0, cols, n).wait_recv())
        pl.when(row < n_row - 1)(lambda: halo(i, field, edges, 1, cols, n).wait_recv())

    def halo_sent(i, field, edges, cols, n):
        pl.when(row < n_row - 1)(lambda: halo(i, field, edges, 0, cols, n).wait_send())
        pl.when(row > 0)(lambda: halo(i, field, edges, 1, cols, n).wait_send())

    def gather(i, cols, n):
        return remote(
            right.at[i, :, cols], right_in.at[i, :, cols], gather_s.at[i, n], gather_r.at[i, n], mate(i)
        )

    for part in range(parts):
        hop_received(n_col - 2, part)
        if part == 0:
            cot_start(n_col - 1)
        rows = slice(part * part_rows, (part + 1) * part_rows)

        @pl.loop(0, n_tiles)
        def _(n):
            cols = aligned(n, tile)

            @pl.when(at_end)
            def _():
                wide[rows, cols] = wide[rows, cols] + jnp.dot(
                    xg[rows, aligned(last, local)], upw[aligned(last, local), cols], preferred_element_type=f32
                )

            hid[rows, cols] = wide[rows, cols].astype(bf16)
            for side, ready in ((1, part == (edge - 1) // part_rows), (0, part == parts - 1)):
                if ready:
                    halo_start(0, hid, hid_halo, side, cols, n)

    for i in (5, 6, 7):
        loads[i].wait()

    def waves_of(matrix, field, cols):
        return jnp.dot(matrix[...], field[:, cols], preferred_element_type=f32)

    def own_waves(waves, field, cols):
        waves[:, cols] = waves_of(fwd_own, field, cols)

    each(n_tiles, lambda n: own_waves(hid_waves, hid, aligned(n, tile)))

    half_waves = tap_waves.shape[0] // 2

    def product(left, other, cols, conjugate):
        lr, li = left[0:half_waves, cols], left[half_waves : 2 * half_waves, cols]
        rr, ri = other[0:half_waves, cols], other[half_waves : 2 * half_waves, cols]
        if conjugate:
            return jnp.concatenate([(lr * rr + li * ri).astype(bf16), (li * rr - lr * ri).astype(bf16)])
        return jnp.concatenate([(lr * rr - li * ri).astype(bf16), (li * rr + lr * ri).astype(bf16)])

    each(n_tiles, lambda n: halo_received(0, hid, hid_halo, aligned(n, tile), n))
    for n in range(n_tiles):
        cols = slice(n * tile, (n + 1) * tile)
        hid_waves[:, cols] = hid_waves[:, cols] + waves_of(fwd_halo, hid_halo, cols)
        preact = jnp.dot(inv[...], product(hid_waves, tap_waves, cols, True), preferred_element_type=f32)
        wide[:, cols] = preact
        act[:, cols] = (preact * jax.nn.sigmoid(preact)).astype(bf16)
        gather(0, cols, n).start()

    pl.when(at_end)(lambda: turn(1, xg, last))

    def project(left, weight, dest, out):
        @pl.loop(0, local // wtile)
        def _(n):
            rows = pl.ds(pl.multiple_of(dest * local + n * wtile, wtile), wtile)
            out[:, aligned(n, wtile)] = lax.dot_general(
                left[...], weight[rows, :], (((1,), (1,)), ((), ())), preferred_element_type=f32
            ).astype(out.dtype)

    def partial(i, dest, source, part):
        rows = slice(part * part_rows, (part + 1) * part_rows)
        return remote(
            sent.at[i, dest, rows], got.at[i, source, rows], sum_out_s.at[i, dest, part], sum_out_r.at[i, source, part],
            {"col": dest},
        )

    def passed(i, side, part):
        rows = slice(part * part_rows, (part + 1) * part_rows)
        return remote(
            sent.at[i, 0 if side else n_col - 1, rows], relay.at[i, side, rows],
            sum_out_s.at[i, 0 if side else n_col - 1, part], relay_r.at[i, side, part],
            {"col": n_col - 2 if side else 1},
        )

    def targets(m):
        far = n_col - 1 - m
        return (
            (0, far, far > col, jnp.logical_and(far == n_col - 1, col == 0), jnp.logical_and(far == n_col - 1, col == 1)),
            (1, m, m < col, jnp.logical_and(m == 0, last == 0), jnp.logical_and(m == 0, last == 1)),
        )

    def sums_begin(i, left, weight):
        @pl.loop(0, n_col - 1)
        def _(m):
            for side, dest, goes, ends, joins in targets(m):
                @pl.when(goes)
                def _():
                    project(left, weight, dest, sent.at[i, dest])
                    for part in range(parts):
                        pl.when(ends)(lambda: passed(i, side, part).start())
                        now = jnp.logical_not(jnp.logical_or(joins, at_end))
                        pl.when(now)(lambda: partial(i, dest, col, part).start())

    def sums_rest(i):
        @pl.when(at_end)
        def _():
            @pl.loop(0, n_col - 1)
            def _(m):
                for side, dest, goes, ends, _ in targets(m):
                    @pl.when(jnp.logical_and(goes, jnp.logical_not(ends)))
                    def _():
                        for part in range(parts):
                            partial(i, dest, col, part).start()

    def sums_join(i):
        for part in range(parts):
            rows = slice(part * part_rows, (part + 1) * part_rows)
            for side, dest, joins in ((0, n_col - 1, col == 1), (1, 0, last == 1)):
                @pl.when(joins)
                def _():
                    passed(i, side, part).wait_recv()
                    total = sent[i, dest, rows].astype(f32) + relay[i, side, rows].astype(f32)
                    sent[i, dest, rows] = total.astype(bf16)
                    partial(i, dest, col, part).start()

    def sums_end(i, residual, out):
        @pl.loop(0, n_col)
        def _(k):
            ends = jnp.logical_or(jnp.logical_and(k == 0, last == 0), jnp.logical_and(k == n_col - 1, col == 0))

            @pl.when(jnp.logical_and(k != col, jnp.logical_not(ends)))
            def _():
                for part in range(parts):
                    partial(i, col, k, part).wait_recv()
                own_sum[i] = own_sum[i] + got[i, k].astype(f32)

        out[...] = (residual[:, mine].astype(f32) + own_sum[i]).astype(bf16)

    def sums_sent(i):
        @pl.loop(0, n_col)
        def _(k):
            @pl.when(k != col)
            def _():
                for part in range(parts):
                    partial(i, k, col, part).wait_send()

    loads[4].wait()
    sums_begin(0, act, dnw)

    @pl.loop(0, n_col)
    def _(k):
        pl.when(k != col)(lambda: cot_copy(col, k).wait_recv())

    @pl.loop(0, n_tiles)
    def _(n):
        cols = aligned(n, tile)
        act_grad = jnp.dot(cg[...], dnw[:, cols], preferred_element_type=f32)
        preact = wide[:, cols]
        logistic = jax.nn.sigmoid(preact)
        grd[:, cols] = (act_grad * logistic * (1.0 + preact * (1.0 - logistic))).astype(bf16)
        halo_start(1, grd, grd_halo, 1, cols, n)
        halo_start(1, grd, grd_halo, 0, cols, n)

    sums_rest(0)
    each(n_col, lambda k: pl.when(k != col)(lambda: turn(0, cg, k)))
    each(n_tiles, lambda n: own_waves(grd_waves, grd, aligned(n, tile)))
    loads[9].wait()

    @pl.loop(0, n_tiles)
    def _(n):
        cols = aligned(n, tile)
        taps_out[:, cols] = jnp.dot(
            inv_taps[...], product(hid_waves, grd_waves, cols, True), preferred_element_type=f32
        ).astype(bf16)

    some, others = aligned(dp, channels // 2), aligned(1 - dp, channels // 2)
    whole_taps = remote(taps_out.at[:, others], taps_in, kg_s.at[0], kg_r.at[0], partner)
    whole_taps.start()
    project(act, dnw, col, own_sum.at[0])
    sums_join(0)

    each(n_tiles, lambda n: halo_received(1, grd, grd_halo, aligned(n, tile), n))
    for n in range(n_tiles):
        cols = slice(n * tile, (n + 1) * tile)
        grd_waves[:, cols] = grd_waves[:, cols] + waves_of(fwd_halo, grd_halo, cols)
        hgr[:, cols] = jnp.dot(
            inv[...], product(grd_waves, tap_waves, cols, False), preferred_element_type=f32
        ).astype(bf16)
        gather(1, cols, n).start()

    sums_begin(1, hgr, upw)

    def pair(i, j, cols, n):
        return remote(first_out.at[i, j, :, cols], first_in.at[i, j, :, cols], pair_s.at[i, j, n], pair_r.at[i, j, n], partner)

    def row_copy(i, to, source, cols, n):
        return remote(
            second_out.at[i, to, :, cols], second_in.at[i, source, :, cols], row_s.at[i, to, n], row_r.at[i, source, n],
            {"row": row_of(i, side_of(i, row), to)},
        )

    def outer(i, half, j, cols):
        index = half * n_row + row_of(i, side_of(i, row), j)
        return jnp.dot(
            turned[i, aligned(index, share)], right[i, :, cols], preferred_element_type=f32
        ) + jnp.dot(turned_in[i, half * n_half + j], right_in[i, :, cols], preferred_element_type=f32)

    def grad_for_partner(i, n):
        cols = aligned(n, tile)
        gather(i, cols, n).wait_recv()

        for j in range(n_half):
            first_out[i, j, :, cols] = outer(i, 1 - dp, j, cols).astype(bf16)
        for j in range(n_half):
            pair(i, j, cols, n).start()

    def grad_own(i, n):
        cols = aligned(n, tile)
        here = place_of(i, row)

        for j in range(n_half):
            pair(i, j, cols, n).wait_recv()
        for j in range(n_half):
            total = outer(i, dp, j, cols) + first_in[i, j, :, cols].astype(f32)
            second_out[i, j, :, cols] = total.astype(bf16)
        if i:
            rows_start(i, n)

    def rows_start(i, n):
        here = place_of(i, row)
        each(n_half, lambda j: pl.when(j != here)(lambda: row_copy(i, j, here, aligned(n, tile), n).start()))

    def grad_step(i, step):
        pl.when(step < n_tiles)(lambda: grad_for_partner(i, step))
        pl.when(jnp.logical_and(step > 0, step <= n_tiles))(lambda: grad_own(i, step - 1))

    def grad_finish(i, out):
        here = place_of(i, row)

        @pl.loop(0, n_tiles)
        def _(n):
            cols = aligned(n, tile)
            own_sum_tile = second_out[i, here, :, cols].astype(f32)
            for k in range(1, n_half):
                source = lax.rem(here + k, n_half)
                row_copy(i, here, source, cols, n).wait_recv()
                own_sum_tile = own_sum_tile + second_in[i, source, :, cols].astype(f32)
            out[:, cols] = own_sum_tile.astype(bf16)

    def pieces_received(i):
        @pl.loop(0, n_dp * n_half)
        def _(slot):
            index = (slot // n_half) * n_row + row_of(i, 1 - side_of(i, row), lax.rem(slot, n_half))
            piece(i, index).wait_recv()

    pieces_received(0)
    each(n_tiles + 1, lambda step: grad_step(0, step))
    sums_rest(1)
    whole_taps.wait_recv()
    share_out[...] = (taps_out[:, some].astype(f32) + taps_in[...].astype(f32)).astype(bf16)
    tap_share = share_out.shape[0] // n_row

    def taps_copy(k):
        peer = lax.rem(row + k, n_row)
        return remote(share_out.at[aligned(peer, tap_share)], share_in.at[k], kg_s.at[k], kg_r.at[k], {"row": peer})

    def taps_sum(k, source):
        target = half_out.at[aligned(source, tap_share)]
        return remote(
            half_out.at[aligned(row, tap_share)], target, sum_s.at[k], sum_r.at[k], {"row": lax.rem(row + k, n_row)}
        )

    each(n_row, lambda k: taps_copy(k).start(), 1)
    sums_end(0, xg, block_output)
    sums_join(1)
    project(hgr, upw, col, own_sum.at[1])
    pieces_received(1)

    @pl.loop(0, n_tiles + 1)
    def _(step):
        grad_step(1, step)
        pl.when(step < n_tiles)(lambda: rows_start(0, step))

    each(n_row, lambda k: taps_copy(k).wait_recv(), 1)
    my_taps = aligned(row, tap_share)
    total = share_out[my_taps].astype(f32)
    for k in range(1, n_row):
        total = total + share_in[k].astype(f32)
    half_out[my_taps] = total.astype(bf16)
    each(n_row, lambda k: taps_sum(k, row).start(), 1)
    grad_finish(0, down_grad)
    each(n_row, lambda k: taps_sum(k, lax.rem(row + n_row - k, n_row)).wait_recv(), 1)
    halves = remote(half_out, half_in, kg_s.at[n_row], kg_r.at[n_row], partner)
    halves.start()
    n_taps = kernel.shape[0]
    kernel_grad[:, some] = half_out[...].astype(f32)[0:n_taps]
    grad_finish(1, up_grad)
    sums_end(1, cg, input_grad)
    halves.wait_recv()
    kernel_grad[:, others] = half_in[...].astype(f32)[0:n_taps]

    for step in range(n_col - 1):
        for part in range(parts):
            for side in (1, -1):
                pl.when(hop_goes(side, step))(hop(side, step, part).wait_send)
    each(n_col, lambda k: pl.when(k != col)(lambda: cot_copy(k, col).wait_send()))
    for i in range(2):
        sums_sent(i)
        each(n_dp * n_row, lambda k: pl.when(leaves(i, k))(lambda: piece(i, k).wait_send()))

        @pl.loop(0, n_tiles)
        def _(n):
            cols = aligned(n, tile)
            halo_sent(i, (hid, grd)[i], (hid_halo, grd_halo)[i], cols, n)
            gather(i, cols, n).wait_send()
            here = place_of(i, row)
            for j in range(n_half):
                pair(i, j, cols, n).wait_send()
                pl.when(j != here)(lambda: row_copy(i, j, here, cols, n).wait_send())

    whole_taps.wait_send()
    each(n_row, lambda k: taps_copy(k).wait_send(), 1)
    each(n_row, lambda k: taps_sum(k, row).wait_send(), 1)
    halves.wait_send()


def hand_on(*refs):
    arrived, done = refs[15], refs[16]
    fetches = [pltpu.make_async_copy(refs[i], refs[10 + i], arrived.at[i]) for i in range(5)]
    stores = [pltpu.make_async_copy(refs[10 + i], refs[5 + i], done.at[i]) for i in range(5)]
    for fetch in fetches:
        fetch.start()
    for fetch, store in zip(fetches, stores):
        fetch.wait()
        store.start()
    for store in stores:
        store.wait()


def on_device(inputs, up_weight, down_weight, kernel, cotangent):
    _, planes, tile_x, tile_y, local = inputs.shape
    n_dp, n_row, n_col = (lax.axis_size(name) for name in ("dp", "row", "col"))
    voxels = planes * tile_x * tile_y
    extended = voxels + 2 * HALO * tile_x * tile_y
    width, channels = up_weight.shape
    share = width // (n_dp * n_row)
    bf16, f32 = jnp.bfloat16, jnp.float32
    dma = pltpu.SemaphoreType.DMA
    taps = kernel.shape[0]
    tap_rows = -(-taps // (16 * n_row)) * 16 * n_row
    vmem, anywhere = pl.BlockSpec(memory_space=pltpu.VMEM), pl.BlockSpec(memory_space=pl.ANY)
    matrices = transforms(planes, tile_x, tile_y, tap_rows)
    n_waves = matrices[0].shape[0]
    tile = min(256, channels)
    n_tiles = channels // tile
    edge = HALO * tile_x * tile_y
    n_half = n_row // 2
    parts = 2 if n_col <= 4 else 1
    outs = pl.pallas_call(
        functools.partial(block_kernel, (planes, tile_x, tile_y, n_dp, n_row, n_col)),
        out_shape=(
            jax.ShapeDtypeStruct((voxels, local), bf16),
            jax.ShapeDtypeStruct((voxels, local), bf16),
            jax.ShapeDtypeStruct((share, channels), bf16),
            jax.ShapeDtypeStruct((share, channels), bf16),
            jax.ShapeDtypeStruct((taps, channels), f32),
        ),
        in_specs=[anywhere] * 10,
        out_specs=(vmem,) * 5,
        scratch_shapes=[
            pltpu.VMEM(kernel.shape, f32),
            pltpu.VMEM((voxels, width), bf16),
            pltpu.VMEM((voxels, width), bf16),
            pltpu.VMEM((width, channels), bf16),
            pltpu.VMEM((width, channels), bf16),
            pltpu.VMEM((voxels, channels), bf16),
            pltpu.VMEM((voxels, channels), bf16),
            pltpu.VMEM((2 * edge, channels), bf16),
            pltpu.VMEM((2 * edge, channels), bf16),
            pltpu.VMEM((voxels, channels), f32),
            pltpu.VMEM((2, voxels, channels), bf16),
            pltpu.VMEM((2, voxels, channels), bf16),
            *(pltpu.VMEM(m.shape, bf16) for m in matrices),
            pltpu.VMEM((n_waves, channels), f32),
            pltpu.VMEM((n_waves, channels), f32),
            pltpu.VMEM((n_waves, channels), f32),
            pltpu.VMEM((2, n_col, voxels, local), bf16),
            pltpu.VMEM((2, n_col, voxels, local), bf16),
            pltpu.VMEM((2, 2, voxels, local), bf16),
            pltpu.VMEM((2, voxels, local), f32),
            pltpu.VMEM((2, width, voxels), bf16),
            pltpu.VMEM((2, n_dp * n_half, share, voxels), bf16),
            pltpu.VMEM((2, n_half, share, channels), bf16),
            pltpu.VMEM((2, n_half, share, channels), bf16),
            pltpu.VMEM((2, n_half, share, channels), bf16),
            pltpu.VMEM((2, n_half, share, channels), bf16),
            pltpu.VMEM((tap_rows, channels), bf16),
            pltpu.VMEM((tap_rows, channels // 2), bf16),
            pltpu.VMEM((tap_rows, channels // 2), bf16),
            pltpu.VMEM((n_row, tap_rows // n_row, channels // 2), bf16),
            pltpu.VMEM((tap_rows, channels // 2), bf16),
            pltpu.VMEM((tap_rows, channels // 2), bf16),
            dma((10,)),
            dma((2, n_col, parts)), dma((2, n_col, parts)),
            dma((n_col,)), dma((n_col,)),
            dma((2, 2, n_tiles)), dma((2, 2, n_tiles)),
            dma((2, n_col, parts)), dma((2, n_col, parts)), dma((2, 2, parts)),
            dma((2, n_dp * n_half)), dma((2, n_dp * n_half)),
            dma((2, n_tiles)), dma((2, n_tiles)),
            dma((2, n_half, n_tiles)), dma((2, n_half, n_tiles)),
            dma((2, n_half, n_tiles)), dma((2, n_half, n_tiles)),
            dma((n_row + 1,)), dma((n_row + 1,)),
            dma((n_row,)), dma((n_row,)),
        ],
        compiler_params=pltpu.CompilerParams(
            collective_id=0, has_side_effects=True, vmem_limit_bytes=60 << 20
        ),
    )(inputs.reshape(voxels, local), cotangent.reshape(voxels, local), up_weight, down_weight, kernel,
      *map(jnp.asarray, matrices))
    outs = pl.pallas_call(
        hand_on,
        out_shape=tuple(jax.ShapeDtypeStruct(out.shape, out.dtype) for out in outs),
        in_specs=[anywhere] * 5,
        out_specs=(anywhere,) * 5,
        scratch_shapes=[pltpu.VMEM(out.shape, out.dtype) for out in outs] + [dma((5,)), dma((5,))],
    )(*outs)
    return (outs[0].reshape(inputs.shape), outs[1].reshape(inputs.shape)) + tuple(outs[2:])


def solution(mesh):
    placed = (
        P("dp", "row", None, None, "col"),
        P(None, "col"),
        P(None, "col"),
        P(None, "col"),
        P("dp", "row", None, None, "col"),
    )
    return jax.shard_map(
        on_device,
        mesh=mesh,
        in_specs=placed,
        out_specs=(
            P("dp", "row", None, None, "col"),
            P("dp", "row", None, None, "col"),
            P(("dp", "row"), "col"),
            P(("dp", "row"), "col"),
            P(None, "col"),
        ),
        check_vma=False,
    )
```

```python
import functools

import jax
import jax.numpy as jnp
import ml_dtypes
import numpy as np
from jax import lax
from jax.experimental import pallas as pl
from jax.experimental.pallas import tpu as pltpu
from jax.sharding import PartitionSpec as P

HALO = 2


def aligned(index, size):
    return pl.ds(pl.multiple_of(index * size, size), size)


def transforms(planes, tile_x, tile_y, tap_rows):
    lengths = np.array([planes + 2 * HALO, tile_x + HALO, tile_y + HALO])
    waves = np.stack([m.ravel() for m in np.meshgrid(*map(np.arange, lengths), indexing="ij")], 1)
    mirrored = (-waves) % lengths
    code = waves @ np.array([lengths[1] * lengths[2], lengths[2], 1])
    mirrored_code = mirrored @ np.array([lengths[1] * lengths[2], lengths[2], 1])
    kept = code <= mirrored_code
    waves, weight = waves[kept], np.where(code == mirrored_code, 1.0, 2.0)[kept] / lengths.prod()
    rows = -(-len(waves) // 16) * 16

    def wave_matrix(*ranges):
        points = np.stack([m.ravel() for m in np.meshgrid(*ranges, indexing="ij")], 1)
        angle = 2 * np.pi * (waves / lengths) @ points.T
        both = np.zeros((2, rows, len(points)))
        both[0, : len(waves)], both[1, : len(waves)] = np.cos(angle), -np.sin(angle)
        return both

    weights = np.zeros(rows)
    weights[: len(waves)] = weight

    def forward(both):
        return both.reshape(2 * rows, -1)

    def backward(both):
        return (both * weights[:, None]).reshape(2 * rows, -1).T

    depth, along_x, along_y = np.arange(planes + 2 * HALO), np.arange(tile_x), np.arange(tile_y)
    reach = np.arange(-HALO, HALO + 1)
    grid = wave_matrix(depth, along_x, along_y)
    own = wave_matrix(depth[HALO:-HALO], along_x, along_y)
    taps = wave_matrix(reach, reach, reach)
    bf16 = ml_dtypes.bfloat16
    taps_high = forward(taps).astype(bf16)
    taps_low = (forward(taps) - taps_high.astype(np.float64)).astype(bf16)
    taps_back = backward(taps)
    taps_back = np.concatenate([taps_back, np.zeros((tap_rows - len(taps_back), taps_back.shape[1]))])
    edge = HALO * tile_x * tile_y
    to_waves = forward(grid)
    return tuple(
        m.astype(bf16)
        for m in (
            to_waves[:, edge:-edge], np.concatenate([to_waves[:, :edge], to_waves[:, -edge:]], 1),
            backward(own), np.stack([taps_high, taps_low]), taps_back,
        )
    )


def block_kernel(
    sizes, inputs, cotangent, up_weight, down_weight, stencil_weights,
    own_to_waves, halo_to_waves, from_waves, taps_to_waves, taps_from_waves,
    block_output_ref, input_grad_ref, up_grad_ref, down_grad_ref, kernel_grad_ref,
    block_output, input_grad, up_grad, down_grad, kernel_grad,
    kernel, xg, cg, upw, dnw, hid, grd, hid_halo, grd_halo, wide, right, right_in,
    fwd_own, fwd_halo, inv, fwd_taps, inv_taps, tap_waves, hid_waves, grd_waves,
    sent, got, relay, own_sum, turned, turned_in, first_out, first_in, second_out, second_in,
    taps_out, taps_in, share_out, share_in, half_out, half_in,
    load_sem, store_sem, ag_s, ag_r, cot_s, cot_r, halo_s, halo_r, sum_out_s, sum_out_r, relay_r, piece_s, piece_r,
    gather_s, gather_r, pair_s, pair_r, row_s, row_r, kg_s, kg_r, sum_s, sum_r,
):
    planes, tile_x, tile_y, n_dp, n_row, n_col = sizes
    dp, row, col = lax.axis_index("dp"), lax.axis_index("row"), lax.axis_index("col")
    partner = {"dp": 1 - dp}
    voxels, local = inputs.shape
    channels = kernel.shape[1]
    edge = HALO * tile_x * tile_y
    tile = min(256, channels)
    n_tiles = channels // tile
    wtile = min(256, local)
    parts = ag_s.shape[2]
    part_rows = voxels // parts
    n_half = n_row // 2
    share = first_out.shape[2]
    bf16, f32 = jnp.bfloat16, jnp.float32
    mine = aligned(col, local)
    act, hgr = right.at[0], right.at[1]

    loads = [
        pltpu.make_async_copy(source, target, load_sem.at[i])
        for i, (source, target) in enumerate((
            (inputs, xg.at[:, mine]), (up_weight, upw), (stencil_weights, kernel), (cotangent, cg.at[:, mine]),
            (down_weight, dnw), (own_to_waves, fwd_own), (halo_to_waves, fwd_halo), (from_waves, inv),
            (taps_to_waves, fwd_taps), (taps_from_waves, inv_taps),
        ))
    ]
    for i in (0, 2, 8, 1, 5, 6, 7, 3, 4, 9):
        loads[i].start()

    stores = [
        pltpu.make_async_copy(source, target, store_sem.at[i])
        for i, (source, target) in enumerate((
            (block_output, block_output_ref), (input_grad, input_grad_ref), (up_grad, up_grad_ref),
            (down_grad, down_grad_ref), (kernel_grad, kernel_grad_ref),
        ))
    ]
    barrier = pltpu.get_barrier_semaphore()

    for side in (1, -1):
        @pl.when(jnp.logical_and(col + side >= 0, col + side < n_col))
        def _():
            pl.semaphore_signal(barrier, inc=1, device_id={"col": col + side})

    @pl.loop(1, n_row)
    def _(k):
        pl.semaphore_signal(barrier, inc=1, device_id={"row": lax.rem(row + k, n_row)})

    pl.semaphore_signal(barrier, inc=1, device_id=partner)
    ends = jnp.where(col == 0, 1, 0) + jnp.where(col == n_col - 1, 1, 0)
    pl.semaphore_wait(barrier, n_row + 2 - ends)

    def remote(source, target, send, receive, device):
        return pltpu.make_async_remote_copy(
            src_ref=source, dst_ref=target, send_sem=send, recv_sem=receive,
            device_id=device, device_id_type=pl.DeviceIdType.MESH,
        )

    def each(count, action, first=0):
        @pl.loop(first, count)
        def _(k):
            action(k)

    def inside(index):
        return jnp.logical_and(index >= 0, index < n_col)

    def hop(side, step, part):
        rows = slice(part * part_rows, (part + 1) * part_rows)
        place = xg.at[rows, aligned(col - side * step, local)]
        return remote(
            inputs.at[rows] if step == 0 else place, place,
            ag_s.at[(side + 1) // 2, step, part], ag_r.at[(side + 1) // 2, step, part], {"col": col + side},
        )

    def hop_goes(side, step):
        return jnp.logical_and(inside(col + side), inside(col - side * step))

    def hop_start(step, part):
        for side in (1, -1):
            pl.when(hop_goes(side, step))(hop(side, step, part).start)

    def hop_received(step, part):
        for side in (1, -1):
            pl.when(inside(col - side * (step + 1)))(hop(side, step, part).wait_recv)

    def cot_copy(peer, source):
        return remote(cotangent, cg.at[:, aligned(source, local)], cot_s.at[peer], cot_r.at[source], {"col": peer})

    def cot_start(slot):
        pl.when(slot > col)(lambda: cot_copy(slot, col).start())
        pl.when(n_col - 1 - slot < col)(lambda: cot_copy(n_col - 1 - slot, col).start())

    def side_of(i, r):
        return r // n_half if i == 0 else lax.rem(r, 2)

    def place_of(i, r):
        return lax.rem(r, n_half) if i == 0 else r // 2

    def row_of(i, side, place):
        return side * n_half + place if i == 0 else 2 * place + side

    def mate(i):
        return {"row": row_of(i, 1 - side_of(i, row), place_of(i, row))}

    def piece(i, index):
        slot = (index // n_row) * n_half + place_of(i, lax.rem(index, n_row))
        return remote(
            turned.at[i, aligned(index, share)], turned_in.at[i, slot], piece_s.at[i, slot], piece_r.at[i, slot], mate(i)
        )

    def leaves(i, index):
        return side_of(i, lax.rem(index, n_row)) != side_of(i, row)

    def turn(i, field, shard):
        turned[i, aligned(shard, local)] = field[:, aligned(shard, local)].T
        for k in range(local // share):
            index = shard * (local // share) + k
            pl.when(leaves(i, index))(lambda: piece(i, index).start())

    hop_start(0, 0)

    def zero_edges(side):
        for halo in (hid_halo, grd_halo):
            halo[side * edge : (side + 1) * edge] = jnp.zeros((edge, channels), bf16)

    pl.when(row == 0)(lambda: zero_edges(0))
    pl.when(row == n_row - 1)(lambda: zero_edges(1))
    loads[2].wait()
    loads[8].wait()

    @pl.loop(0, n_tiles)
    def _(n):
        cols = aligned(n, tile)
        weights = kernel[:, cols]
        high = weights.astype(bf16)
        low = (weights - high.astype(f32)).astype(bf16)
        tap_waves[:, cols] = (
            jnp.dot(fwd_taps[0], high, preferred_element_type=f32)
            + jnp.dot(fwd_taps[1], high, preferred_element_type=f32)
            + jnp.dot(fwd_taps[0], low, preferred_element_type=f32)
        )

    for part in range(1, parts):
        hop_start(0, part)
    loads[0].wait()
    loads[1].wait()

    def expand(shard, cols):
        return jnp.dot(xg[:, aligned(shard, local)], upw[aligned(shard, local), cols], preferred_element_type=f32)

    @pl.loop(0, n_tiles)
    def _(n):
        cols = aligned(n, tile)
        wide[:, cols] = expand(col, cols)

    turn(1, xg, col)
    loads[3].wait()
    turn(0, cg, col)
    for slot in range(1, n_col - 1):
        for part in range(parts):
            hop_received(slot - 1, part)
            hop_start(slot, part)
        cot_start(slot)
        for side in (1, -1):
            shard = col - side * slot

            @pl.when(inside(shard))
            def _():
                @pl.loop(0, n_tiles)
                def _(n):
                    cols = aligned(n, tile)
                    wide[:, cols] = wide[:, cols] + expand(shard, cols)

                turn(1, xg, shard)

    last = n_col - 1 - col
    at_end = jnp.logical_or(col == 0, last == 0)

    def halo(i, field, edges, side, cols, n):
        if side:
            source, target, peer = 0, edge, row - 1
        else:
            source, target, peer = voxels - edge, 0, row + 1
        return remote(
            field.at[source : source + edge, cols], edges.at[target : target + edge, cols],
            halo_s.at[i, side, n], halo_r.at[i, side, n], {"row": peer},
        )

    def halo_start(i, field, edges, side, cols, n):
        pl.when(row > 0 if side else row < n_row - 1)(lambda: halo(i, field, edges, side, cols, n).start())

    def halo_received(i, field, edges, cols, n):
        pl.when(row > 0)(lambda: halo(i, field, edges, 0, cols, n).wait_recv())
        pl.when(row < n_row - 1)(lambda: halo(i, field, edges, 1, cols, n).wait_recv())

    def halo_sent(i, field, edges, cols, n):
        pl.when(row < n_row - 1)(lambda: halo(i, field, edges, 0, cols, n).wait_send())
        pl.when(row > 0)(lambda: halo(i, field, edges, 1, cols, n).wait_send())

    def gather(i, cols, n):
        return remote(
            right.at[i, :, cols], right_in.at[i, :, cols], gather_s.at[i, n], gather_r.at[i, n], mate(i)
        )

    for part in range(parts):
        hop_received(n_col - 2, part)
        if part == 0:
            cot_start(n_col - 1)
        rows = slice(part * part_rows, (part + 1) * part_rows)

        @pl.loop(0, n_tiles)
        def _(n):
            cols = aligned(n, tile)

            @pl.when(at_end)
            def _():
                wide[rows, cols] = wide[rows, cols] + jnp.dot(
                    xg[rows, aligned(last, local)], upw[aligned(last, local), cols], preferred_element_type=f32
                )

            hid[rows, cols] = wide[rows, cols].astype(bf16)
            for side, ready in ((1, part == (edge - 1) // part_rows), (0, part == parts - 1)):
                if ready:
                    halo_start(0, hid, hid_halo, side, cols, n)

    for i in (5, 6, 7):
        loads[i].wait()

    def waves_of(matrix, field, cols):
        return jnp.dot(matrix[...], field[:, cols], preferred_element_type=f32)

    def own_waves(waves, field, cols):
        waves[:, cols] = waves_of(fwd_own, field, cols)

    each(n_tiles, lambda n: own_waves(hid_waves, hid, aligned(n, tile)))

    half_waves = tap_waves.shape[0] // 2

    def product(left, other, cols, conjugate):
        lr, li = left[0:half_waves, cols], left[half_waves : 2 * half_waves, cols]
        rr, ri = other[0:half_waves, cols], other[half_waves : 2 * half_waves, cols]
        if conjugate:
            return jnp.concatenate([(lr * rr + li * ri).astype(bf16), (li * rr - lr * ri).astype(bf16)])
        return jnp.concatenate([(lr * rr - li * ri).astype(bf16), (li * rr + lr * ri).astype(bf16)])

    each(n_tiles, lambda n: halo_received(0, hid, hid_halo, aligned(n, tile), n))
    for n in range(n_tiles):
        cols = slice(n * tile, (n + 1) * tile)
        hid_waves[:, cols] = hid_waves[:, cols] + waves_of(fwd_halo, hid_halo, cols)
        preact = jnp.dot(inv[...], product(hid_waves, tap_waves, cols, True), preferred_element_type=f32)
        wide[:, cols] = preact
        act[:, cols] = (preact * jax.nn.sigmoid(preact)).astype(bf16)
        gather(0, cols, n).start()

    pl.when(at_end)(lambda: turn(1, xg, last))

    def project(left, weight, dest, out):
        @pl.loop(0, local // wtile)
        def _(n):
            rows = pl.ds(pl.multiple_of(dest * local + n * wtile, wtile), wtile)
            out[:, aligned(n, wtile)] = lax.dot_general(
                left[...], weight[rows, :], (((1,), (1,)), ((), ())), preferred_element_type=f32
            ).astype(out.dtype)

    def partial(i, dest, source, part):
        rows = slice(part * part_rows, (part + 1) * part_rows)
        return remote(
            sent.at[i, dest, rows], got.at[i, source, rows], sum_out_s.at[i, dest, part], sum_out_r.at[i, source, part],
            {"col": dest},
        )

    def passed(i, side, part):
        rows = slice(part * part_rows, (part + 1) * part_rows)
        return remote(
            sent.at[i, 0 if side else n_col - 1, rows], relay.at[i, side, rows],
            sum_out_s.at[i, 0 if side else n_col - 1, part], relay_r.at[i, side, part],
            {"col": n_col - 2 if side else 1},
        )

    def targets(m):
        far = n_col - 1 - m
        return (
            (0, far, far > col, jnp.logical_and(far == n_col - 1, col == 0), jnp.logical_and(far == n_col - 1, col == 1)),
            (1, m, m < col, jnp.logical_and(m == 0, last == 0), jnp.logical_and(m == 0, last == 1)),
        )

    def sums_begin(i, left, weight):
        @pl.loop(0, n_col - 1)
        def _(m):
            for side, dest, goes, ends, joins in targets(m):
                @pl.when(goes)
                def _():
                    project(left, weight, dest, sent.at[i, dest])
                    for part in range(parts):
                        pl.when(ends)(lambda: passed(i, side, part).start())
                        now = jnp.logical_not(jnp.logical_or(joins, at_end))
                        pl.when(now)(lambda: partial(i, dest, col, part).start())

    def sums_rest(i):
        @pl.when(at_end)
        def _():
            @pl.loop(0, n_col - 1)
            def _(m):
                for side, dest, goes, ends, _ in targets(m):
                    @pl.when(jnp.logical_and(goes, jnp.logical_not(ends)))
                    def _():
                        for part in range(parts):
                            partial(i, dest, col, part).start()

    def sums_join(i):
        for part in range(parts):
            rows = slice(part * part_rows, (part + 1) * part_rows)
            for side, dest, joins in ((0, n_col - 1, col == 1), (1, 0, last == 1)):
                @pl.when(joins)
                def _():
                    passed(i, side, part).wait_recv()
                    total = sent[i, dest, rows].astype(f32) + relay[i, side, rows].astype(f32)
                    sent[i, dest, rows] = total.astype(bf16)
                    partial(i, dest, col, part).start()

    def sums_end(i, residual, out):
        @pl.loop(0, n_col)
        def _(k):
            ends = jnp.logical_or(jnp.logical_and(k == 0, last == 0), jnp.logical_and(k == n_col - 1, col == 0))

            @pl.when(jnp.logical_and(k != col, jnp.logical_not(ends)))
            def _():
                for part in range(parts):
                    partial(i, col, k, part).wait_recv()
                own_sum[i] = own_sum[i] + got[i, k].astype(f32)

        out[...] = (residual[:, mine].astype(f32) + own_sum[i]).astype(bf16)

    def sums_sent(i):
        @pl.loop(0, n_col)
        def _(k):
            @pl.when(k != col)
            def _():
                for part in range(parts):
                    partial(i, k, col, part).wait_send()

    loads[4].wait()
    sums_begin(0, act, dnw)

    @pl.loop(0, n_col)
    def _(k):
        pl.when(k != col)(lambda: cot_copy(col, k).wait_recv())

    @pl.loop(0, n_tiles)
    def _(n):
        cols = aligned(n, tile)
        act_grad = jnp.dot(cg[...], dnw[:, cols], preferred_element_type=f32)
        preact = wide[:, cols]
        logistic = jax.nn.sigmoid(preact)
        grd[:, cols] = (act_grad * logistic * (1.0 + preact * (1.0 - logistic))).astype(bf16)
        halo_start(1, grd, grd_halo, 1, cols, n)
        halo_start(1, grd, grd_halo, 0, cols, n)

    sums_rest(0)
    each(n_col, lambda k: pl.when(k != col)(lambda: turn(0, cg, k)))
    each(n_tiles, lambda n: own_waves(grd_waves, grd, aligned(n, tile)))
    loads[9].wait()

    @pl.loop(0, n_tiles)
    def _(n):
        cols = aligned(n, tile)
        taps_out[:, cols] = jnp.dot(
            inv_taps[...], product(hid_waves, grd_waves, cols, True), preferred_element_type=f32
        ).astype(bf16)

    some, others = aligned(dp, channels // 2), aligned(1 - dp, channels // 2)
    whole_taps = remote(taps_out.at[:, others], taps_in, kg_s.at[0], kg_r.at[0], partner)
    whole_taps.start()
    project(act, dnw, col, own_sum.at[0])
    sums_join(0)

    each(n_tiles, lambda n: halo_received(1, grd, grd_halo, aligned(n, tile), n))
    for n in range(n_tiles):
        cols = slice(n * tile, (n + 1) * tile)
        grd_waves[:, cols] = grd_waves[:, cols] + waves_of(fwd_halo, grd_halo, cols)
        hgr[:, cols] = jnp.dot(
            inv[...], product(grd_waves, tap_waves, cols, False), preferred_element_type=f32
        ).astype(bf16)
        gather(1, cols, n).start()

    sums_begin(1, hgr, upw)

    def pair(i, j, cols, n):
        return remote(first_out.at[i, j, :, cols], first_in.at[i, j, :, cols], pair_s.at[i, j, n], pair_r.at[i, j, n], partner)

    def row_copy(i, to, source, cols, n):
        return remote(
            second_out.at[i, to, :, cols], second_in.at[i, source, :, cols], row_s.at[i, to, n], row_r.at[i, source, n],
            {"row": row_of(i, side_of(i, row), to)},
        )

    def outer(i, half, j, cols):
        index = half * n_row + row_of(i, side_of(i, row), j)
        return jnp.dot(
            turned[i, aligned(index, share)], right[i, :, cols], preferred_element_type=f32
        ) + jnp.dot(turned_in[i, half * n_half + j], right_in[i, :, cols], preferred_element_type=f32)

    def grad_for_partner(i, n):
        cols = aligned(n, tile)
        gather(i, cols, n).wait_recv()

        for j in range(n_half):
            first_out[i, j, :, cols] = outer(i, 1 - dp, j, cols).astype(bf16)
        for j in range(n_half):
            pair(i, j, cols, n).start()

    def grad_own(i, n):
        cols = aligned(n, tile)
        here = place_of(i, row)

        for j in range(n_half):
            pair(i, j, cols, n).wait_recv()
        for j in range(n_half):
            total = outer(i, dp, j, cols) + first_in[i, j, :, cols].astype(f32)
            second_out[i, j, :, cols] = total.astype(bf16)
        if i:
            rows_start(i, n)

    def rows_start(i, n):
        here = place_of(i, row)
        each(n_half, lambda j: pl.when(j != here)(lambda: row_copy(i, j, here, aligned(n, tile), n).start()))

    def grad_step(i, step):
        pl.when(step < n_tiles)(lambda: grad_for_partner(i, step))
        pl.when(jnp.logical_and(step > 0, step <= n_tiles))(lambda: grad_own(i, step - 1))

    def grad_finish(i, out):
        here = place_of(i, row)

        @pl.loop(0, n_tiles)
        def _(n):
            cols = aligned(n, tile)
            own_sum_tile = second_out[i, here, :, cols].astype(f32)
            for k in range(1, n_half):
                source = lax.rem(here + k, n_half)
                row_copy(i, here, source, cols, n).wait_recv()
                own_sum_tile = own_sum_tile + second_in[i, source, :, cols].astype(f32)
            out[:, cols] = own_sum_tile.astype(bf16)

    def pieces_received(i):
        @pl.loop(0, n_dp * n_half)
        def _(slot):
            index = (slot // n_half) * n_row + row_of(i, 1 - side_of(i, row), lax.rem(slot, n_half))
            piece(i, index).wait_recv()

    pieces_received(0)
    each(n_tiles + 1, lambda step: grad_step(0, step))
    sums_rest(1)
    whole_taps.wait_recv()
    share_out[...] = (taps_out[:, some].astype(f32) + taps_in[...].astype(f32)).astype(bf16)
    tap_share = share_out.shape[0] // n_row

    def taps_copy(k):
        peer = lax.rem(row + k, n_row)
        return remote(share_out.at[aligned(peer, tap_share)], share_in.at[k], kg_s.at[k], kg_r.at[k], {"row": peer})

    def taps_sum(k, source):
        target = half_out.at[aligned(source, tap_share)]
        return remote(
            half_out.at[aligned(row, tap_share)], target, sum_s.at[k], sum_r.at[k], {"row": lax.rem(row + k, n_row)}
        )

    each(n_row, lambda k: taps_copy(k).start(), 1)
    sums_end(0, xg, block_output)
    stores[0].start()
    sums_join(1)
    project(hgr, upw, col, own_sum.at[1])
    pieces_received(1)

    @pl.loop(0, n_tiles + 1)
    def _(step):
        grad_step(1, step)
        pl.when(step < n_tiles)(lambda: rows_start(0, step))

    each(n_row, lambda k: taps_copy(k).wait_recv(), 1)
    my_taps = aligned(row, tap_share)
    total = share_out[my_taps].astype(f32)
    for k in range(1, n_row):
        total = total + share_in[k].astype(f32)
    half_out[my_taps] = total.astype(bf16)
    each(n_row, lambda k: taps_sum(k, row).start(), 1)
    sums_end(1, cg, input_grad)
    stores[1].start()
    each(n_row, lambda k: taps_sum(k, lax.rem(row + n_row - k, n_row)).wait_recv(), 1)
    halves = remote(half_out, half_in, kg_s.at[n_row], kg_r.at[n_row], partner)
    halves.start()
    n_taps = kernel.shape[0]
    kernel_grad[:, some] = half_out[...].astype(f32)[0:n_taps]
    grad_finish(1, up_grad)
    stores[2].start()
    halves.wait_recv()
    kernel_grad[:, others] = half_in[...].astype(f32)[0:n_taps]
    stores[4].start()
    grad_finish(0, down_grad)
    stores[3].start()

    for step in range(n_col - 1):
        for part in range(parts):
            for side in (1, -1):
                pl.when(hop_goes(side, step))(hop(side, step, part).wait_send)
    each(n_col, lambda k: pl.when(k != col)(lambda: cot_copy(k, col).wait_send()))
    for i in range(2):
        sums_sent(i)
        each(n_dp * n_row, lambda k: pl.when(leaves(i, k))(lambda: piece(i, k).wait_send()))

        @pl.loop(0, n_tiles)
        def _(n):
            cols = aligned(n, tile)
            halo_sent(i, (hid, grd)[i], (hid_halo, grd_halo)[i], cols, n)
            gather(i, cols, n).wait_send()
            here = place_of(i, row)
            for j in range(n_half):
                pair(i, j, cols, n).wait_send()
                pl.when(j != here)(lambda: row_copy(i, j, here, cols, n).wait_send())

    whole_taps.wait_send()
    each(n_row, lambda k: taps_copy(k).wait_send(), 1)
    each(n_row, lambda k: taps_sum(k, row).wait_send(), 1)
    halves.wait_send()
    for store in stores:
        store.wait()


def hand_on(*refs):
    arrived, done = refs[15], refs[16]
    fetches = [pltpu.make_async_copy(refs[i], refs[10 + i], arrived.at[i]) for i in range(5)]
    stores = [pltpu.make_async_copy(refs[10 + i], refs[5 + i], done.at[i]) for i in range(5)]
    for fetch in fetches:
        fetch.start()
    for fetch, store in zip(fetches, stores):
        fetch.wait()
        store.start()
    for store in stores:
        store.wait()


def on_device(inputs, up_weight, down_weight, kernel, cotangent):
    _, planes, tile_x, tile_y, local = inputs.shape
    n_dp, n_row, n_col = (lax.axis_size(name) for name in ("dp", "row", "col"))
    voxels = planes * tile_x * tile_y
    extended = voxels + 2 * HALO * tile_x * tile_y
    width, channels = up_weight.shape
    share = width // (n_dp * n_row)
    bf16, f32 = jnp.bfloat16, jnp.float32
    dma = pltpu.SemaphoreType.DMA
    taps = kernel.shape[0]
    tap_rows = -(-taps // (16 * n_row)) * 16 * n_row
    anywhere = pl.BlockSpec(memory_space=pl.ANY)
    matrices = transforms(planes, tile_x, tile_y, tap_rows)
    n_waves = matrices[0].shape[0]
    tile = min(256, channels)
    n_tiles = channels // tile
    edge = HALO * tile_x * tile_y
    n_half = n_row // 2
    parts = 2 if n_col <= 4 else 1
    out_types = (
        ((voxels, local), bf16), ((voxels, local), bf16), ((share, channels), bf16), ((share, channels), bf16),
        ((taps, channels), f32),
    )
    outs = pl.pallas_call(
        functools.partial(block_kernel, (planes, tile_x, tile_y, n_dp, n_row, n_col)),
        out_shape=tuple(jax.ShapeDtypeStruct(shape, dtype) for shape, dtype in out_types),
        in_specs=[anywhere] * 10,
        out_specs=(anywhere,) * 5,
        scratch_shapes=[
            *(pltpu.VMEM(shape, dtype) for shape, dtype in out_types),
            pltpu.VMEM(kernel.shape, f32),
            pltpu.VMEM((voxels, width), bf16),
            pltpu.VMEM((voxels, width), bf16),
            pltpu.VMEM((width, channels), bf16),
            pltpu.VMEM((width, channels), bf16),
            pltpu.VMEM((voxels, channels), bf16),
            pltpu.VMEM((voxels, channels), bf16),
            pltpu.VMEM((2 * edge, channels), bf16),
            pltpu.VMEM((2 * edge, channels), bf16),
            pltpu.VMEM((voxels, channels), f32),
            pltpu.VMEM((2, voxels, channels), bf16),
            pltpu.VMEM((2, voxels, channels), bf16),
            *(pltpu.VMEM(m.shape, bf16) for m in matrices),
            pltpu.VMEM((n_waves, channels), f32),
            pltpu.VMEM((n_waves, channels), f32),
            pltpu.VMEM((n_waves, channels), f32),
            pltpu.VMEM((2, n_col, voxels, local), bf16),
            pltpu.VMEM((2, n_col, voxels, local), bf16),
            pltpu.VMEM((2, 2, voxels, local), bf16),
            pltpu.VMEM((2, voxels, local), f32),
            pltpu.VMEM((2, width, voxels), bf16),
            pltpu.VMEM((2, n_dp * n_half, share, voxels), bf16),
            pltpu.VMEM((2, n_half, share, channels), bf16),
            pltpu.VMEM((2, n_half, share, channels), bf16),
            pltpu.VMEM((2, n_half, share, channels), bf16),
            pltpu.VMEM((2, n_half, share, channels), bf16),
            pltpu.VMEM((tap_rows, channels), bf16),
            pltpu.VMEM((tap_rows, channels // 2), bf16),
            pltpu.VMEM((tap_rows, channels // 2), bf16),
            pltpu.VMEM((n_row, tap_rows // n_row, channels // 2), bf16),
            pltpu.VMEM((tap_rows, channels // 2), bf16),
            pltpu.VMEM((tap_rows, channels // 2), bf16),
            dma((10,)), dma((5,)),
            dma((2, n_col, parts)), dma((2, n_col, parts)),
            dma((n_col,)), dma((n_col,)),
            dma((2, 2, n_tiles)), dma((2, 2, n_tiles)),
            dma((2, n_col, parts)), dma((2, n_col, parts)), dma((2, 2, parts)),
            dma((2, n_dp * n_half)), dma((2, n_dp * n_half)),
            dma((2, n_tiles)), dma((2, n_tiles)),
            dma((2, n_half, n_tiles)), dma((2, n_half, n_tiles)),
            dma((2, n_half, n_tiles)), dma((2, n_half, n_tiles)),
            dma((n_row + 1,)), dma((n_row + 1,)),
            dma((n_row,)), dma((n_row,)),
        ],
        compiler_params=pltpu.CompilerParams(
            collective_id=0, has_side_effects=True, vmem_limit_bytes=60 << 20
        ),
    )(inputs.reshape(voxels, local), cotangent.reshape(voxels, local), up_weight, down_weight, kernel,
      *map(jnp.asarray, matrices))
    outs = pl.pallas_call(
        hand_on,
        out_shape=tuple(jax.ShapeDtypeStruct(out.shape, out.dtype) for out in outs),
        in_specs=[anywhere] * 5,
        out_specs=(anywhere,) * 5,
        scratch_shapes=[pltpu.VMEM(out.shape, out.dtype) for out in outs] + [dma((5,)), dma((5,))],
    )(*outs)
    return (outs[0].reshape(inputs.shape), outs[1].reshape(inputs.shape)) + tuple(outs[2:])


def solution(mesh):
    placed = (
        P("dp", "row", None, None, "col"),
        P(None, "col"),
        P(None, "col"),
        P(None, "col"),
        P("dp", "row", None, None, "col"),
    )
    return jax.shard_map(
        on_device,
        mesh=mesh,
        in_specs=placed,
        out_specs=(
            P("dp", "row", None, None, "col"),
            P("dp", "row", None, None, "col"),
            P(("dp", "row"), "col"),
            P(("dp", "row"), "col"),
            P(None, "col"),
        ),
        check_vma=False,
    )
```

```python
import functools

import jax
import jax.numpy as jnp
import ml_dtypes
import numpy as np
from jax import lax
from jax.experimental import pallas as pl
from jax.experimental.pallas import tpu as pltpu
from jax.sharding import PartitionSpec as P

HALO = 2


def aligned(index, size):
    return pl.ds(pl.multiple_of(index * size, size), size)


def transforms(planes, tile_x, tile_y, tap_rows):
    lengths = np.array([planes + 2 * HALO, tile_x + HALO, tile_y + HALO])
    waves = np.stack([m.ravel() for m in np.meshgrid(*map(np.arange, lengths), indexing="ij")], 1)
    mirrored = (-waves) % lengths
    code = waves @ np.array([lengths[1] * lengths[2], lengths[2], 1])
    mirrored_code = mirrored @ np.array([lengths[1] * lengths[2], lengths[2], 1])
    kept = code <= mirrored_code
    waves, weight = waves[kept], np.where(code == mirrored_code, 1.0, 2.0)[kept] / lengths.prod()
    rows = -(-len(waves) // 16) * 16

    def wave_matrix(*ranges):
        points = np.stack([m.ravel() for m in np.meshgrid(*ranges, indexing="ij")], 1)
        angle = 2 * np.pi * (waves / lengths) @ points.T
        both = np.zeros((2, rows, len(points)))
        both[0, : len(waves)], both[1, : len(waves)] = np.cos(angle), -np.sin(angle)
        return both

    weights = np.zeros(rows)
    weights[: len(waves)] = weight

    def forward(both):
        return both.reshape(2 * rows, -1)

    def backward(both):
        return (both * weights[:, None]).reshape(2 * rows, -1).T

    depth, along_x, along_y = np.arange(planes + 2 * HALO), np.arange(tile_x), np.arange(tile_y)
    reach = np.arange(-HALO, HALO + 1)
    grid = wave_matrix(depth, along_x, along_y)
    own = wave_matrix(depth[HALO:-HALO], along_x, along_y)
    taps = wave_matrix(reach, reach, reach)
    bf16 = ml_dtypes.bfloat16
    taps_high = forward(taps).astype(bf16)
    taps_low = (forward(taps) - taps_high.astype(np.float64)).astype(bf16)
    taps_back = backward(taps)
    taps_back = np.concatenate([taps_back, np.zeros((tap_rows - len(taps_back), taps_back.shape[1]))])
    edge = HALO * tile_x * tile_y
    to_waves = forward(grid)
    return tuple(
        m.astype(bf16)
        for m in (
            to_waves[:, edge:-edge], np.concatenate([to_waves[:, :edge], to_waves[:, -edge:]], 1),
            backward(own), np.stack([taps_high, taps_low]), taps_back,
        )
    )


def block_kernel(
    sizes, inputs, cotangent, up_weight, down_weight, stencil_weights,
    own_to_waves, halo_to_waves, from_waves, taps_to_waves, taps_from_waves,
    block_output_ref, input_grad_ref, up_grad_ref, down_grad_ref, kernel_grad_ref,
    block_output, input_grad, up_grad, down_grad, kernel_grad,
    kernel, xg, cg, upw, dnw, hid, grd, hid_halo, grd_halo, wide, right, right_in,
    fwd_own, fwd_halo, inv, fwd_taps, inv_taps, tap_waves, hid_waves, grd_waves,
    sent, got, relay, own_sum, turned, turned_in, first_out, first_in, second_out, second_in,
    taps_out, taps_in, share_out, share_in, half_out, half_in,
    load_sem, store_sem, ag_s, ag_r, cot_s, cot_r, halo_s, halo_r, sum_out_s, sum_out_r, relay_r, piece_s, piece_r,
    gather_s, gather_r, pair_s, pair_r, row_s, row_r, kg_s, kg_r, sum_s, sum_r,
):
    planes, tile_x, tile_y, n_dp, n_row, n_col = sizes
    dp, row, col = lax.axis_index("dp"), lax.axis_index("row"), lax.axis_index("col")
    partner = {"dp": 1 - dp}
    voxels, local = inputs.shape
    channels = kernel.shape[1]
    edge = HALO * tile_x * tile_y
    tile = min(256, channels)
    n_tiles = channels // tile
    wtile = min(256, local)
    parts = ag_s.shape[2]
    part_rows = voxels // parts
    n_half = n_row // 2
    share = first_out.shape[2]
    bf16, f32 = jnp.bfloat16, jnp.float32
    mine = aligned(col, local)
    act, hgr = right.at[0], right.at[1]

    loads = [
        pltpu.make_async_copy(source, target, load_sem.at[i])
        for i, (source, target) in enumerate((
            (inputs, xg.at[:, mine]), (up_weight, upw), (stencil_weights, kernel), (cotangent, cg.at[:, mine]),
            (down_weight, dnw), (own_to_waves, fwd_own), (halo_to_waves, fwd_halo), (from_waves, inv),
            (taps_to_waves, fwd_taps), (taps_from_waves, inv_taps),
        ))
    ]
    for i in (0, 2, 8, 1, 5, 6, 7, 3, 4, 9):
        loads[i].start()

    stores = [
        pltpu.make_async_copy(source, target, store_sem.at[i])
        for i, (source, target) in enumerate((
            (block_output, block_output_ref), (input_grad, input_grad_ref), (up_grad, up_grad_ref),
            (down_grad, down_grad_ref), (kernel_grad, kernel_grad_ref),
        ))
    ]
    barrier = pltpu.get_barrier_semaphore()

    for side in (1, -1):
        @pl.when(jnp.logical_and(col + side >= 0, col + side < n_col))
        def _():
            pl.semaphore_signal(barrier, inc=1, device_id={"col": col + side})

    near = n_row == 4

    @pl.loop(1, n_row)
    def _(k):
        peer = lax.rem(row + k, n_row)

        @pl.when(jnp.logical_or(not near, peer + row != n_row - 1))
        def _():
            pl.semaphore_signal(barrier, inc=1, device_id={"row": peer})

    pl.semaphore_signal(barrier, inc=1, device_id=partner)
    ends = jnp.where(col == 0, 1, 0) + jnp.where(col == n_col - 1, 1, 0)
    pl.semaphore_wait(barrier, n_row + (1 if near else 2) - ends)

    def remote(source, target, send, receive, device):
        return pltpu.make_async_remote_copy(
            src_ref=source, dst_ref=target, send_sem=send, recv_sem=receive,
            device_id=device, device_id_type=pl.DeviceIdType.MESH,
        )

    def each(count, action, first=0):
        @pl.loop(first, count)
        def _(k):
            action(k)

    def inside(index):
        return jnp.logical_and(index >= 0, index < n_col)

    def hop(side, step, part):
        rows = slice(part * part_rows, (part + 1) * part_rows)
        place = xg.at[rows, aligned(col - side * step, local)]
        return remote(
            inputs.at[rows] if step == 0 else place, place,
            ag_s.at[(side + 1) // 2, step, part], ag_r.at[(side + 1) // 2, step, part], {"col": col + side},
        )

    def hop_goes(side, step):
        return jnp.logical_and(inside(col + side), inside(col - side * step))

    def hop_start(step, part):
        for side in (1, -1):
            pl.when(hop_goes(side, step))(hop(side, step, part).start)

    def hop_received(step, part):
        for side in (1, -1):
            pl.when(inside(col - side * (step + 1)))(hop(side, step, part).wait_recv)

    def cot_copy(peer, source):
        return remote(cotangent, cg.at[:, aligned(source, local)], cot_s.at[peer], cot_r.at[source], {"col": peer})

    def cot_start(slot):
        pl.when(slot > col)(lambda: cot_copy(slot, col).start())
        pl.when(n_col - 1 - slot < col)(lambda: cot_copy(n_col - 1 - slot, col).start())

    def side_of(i, r):
        return r // n_half if i == 0 else lax.rem(r, 2)

    def place_of(i, r):
        return lax.rem(r, n_half) if i == 0 else r // 2

    def row_of(i, side, place):
        return side * n_half + place if i == 0 else 2 * place + side

    def mate(i):
        return {"row": row_of(i, 1 - side_of(i, row), place_of(i, row))}

    def piece(i, index):
        slot = (index // n_row) * n_half + place_of(i, lax.rem(index, n_row))
        return remote(
            turned.at[i, aligned(index, share)], turned_in.at[i, slot], piece_s.at[i, slot], piece_r.at[i, slot], mate(i)
        )

    def leaves(i, index):
        return side_of(i, lax.rem(index, n_row)) != side_of(i, row)

    def is_first(i, index):
        return jnp.logical_and(jnp.logical_not(leaves(i, index)), (index * share) // local == col)

    def turn(i, field, shard):
        turned[i, aligned(shard, local)] = field[:, aligned(shard, local)].T
        for k in range(local // share):
            index = shard * (local // share) + k
            pl.when(leaves(i, index))(lambda: piece(i, index).start())

    hop_start(0, 0)

    def zero_edges(side):
        for halo in (hid_halo, grd_halo):
            halo[side * edge : (side + 1) * edge] = jnp.zeros((edge, channels), bf16)

    pl.when(row == 0)(lambda: zero_edges(0))
    pl.when(row == n_row - 1)(lambda: zero_edges(1))
    loads[2].wait()
    loads[8].wait()

    @pl.loop(0, n_tiles)
    def _(n):
        cols = aligned(n, tile)
        weights = kernel[:, cols]
        high = weights.astype(bf16)
        low = (weights - high.astype(f32)).astype(bf16)
        tap_waves[:, cols] = (
            jnp.dot(fwd_taps[0], high, preferred_element_type=f32)
            + jnp.dot(fwd_taps[1], high, preferred_element_type=f32)
            + jnp.dot(fwd_taps[0], low, preferred_element_type=f32)
        )

    for part in range(1, parts):
        hop_start(0, part)
    loads[0].wait()
    loads[1].wait()

    def expand(shard, cols):
        return jnp.dot(xg[:, aligned(shard, local)], upw[aligned(shard, local), cols], preferred_element_type=f32)

    @pl.loop(0, n_tiles)
    def _(n):
        cols = aligned(n, tile)
        wide[:, cols] = expand(col, cols)

    turn(1, xg, col)
    loads[3].wait()
    turn(0, cg, col)
    for slot in range(1, n_col - 1):
        for part in range(parts):
            hop_received(slot - 1, part)
            hop_start(slot, part)
        cot_start(slot)
        for side in (1, -1):
            shard = col - side * slot

            @pl.when(inside(shard))
            def _():
                @pl.loop(0, n_tiles)
                def _(n):
                    cols = aligned(n, tile)
                    wide[:, cols] = wide[:, cols] + expand(shard, cols)

                turn(1, xg, shard)

    last = n_col - 1 - col
    at_end = jnp.logical_or(col == 0, last == 0)

    def halo(i, field, edges, side, cols, n):
        if side:
            source, target, peer = 0, edge, row - 1
        else:
            source, target, peer = voxels - edge, 0, row + 1
        return remote(
            field.at[source : source + edge, cols], edges.at[target : target + edge, cols],
            halo_s.at[i, side, n], halo_r.at[i, side, n], {"row": peer},
        )

    def halo_start(i, field, edges, side, cols, n):
        pl.when(row > 0 if side else row < n_row - 1)(lambda: halo(i, field, edges, side, cols, n).start())

    def halo_received(i, field, edges, cols, n):
        pl.when(row > 0)(lambda: halo(i, field, edges, 0, cols, n).wait_recv())
        pl.when(row < n_row - 1)(lambda: halo(i, field, edges, 1, cols, n).wait_recv())

    def halo_sent(i, field, edges, cols, n):
        pl.when(row < n_row - 1)(lambda: halo(i, field, edges, 0, cols, n).wait_send())
        pl.when(row > 0)(lambda: halo(i, field, edges, 1, cols, n).wait_send())

    def gather(i, cols, n):
        return remote(
            right.at[i, :, cols], right_in.at[i, :, cols], gather_s.at[i, n], gather_r.at[i, n], mate(i)
        )

    each(n_dp * n_row, lambda k: pl.when(is_first(1, k))(lambda: piece(1, k).wait_recv()))

    for part in range(parts):
        hop_received(n_col - 2, part)
        if part == 0:
            cot_start(n_col - 1)
        rows = slice(part * part_rows, (part + 1) * part_rows)

        @pl.loop(0, n_tiles)
        def _(n):
            cols = aligned(n, tile)

            @pl.when(at_end)
            def _():
                wide[rows, cols] = wide[rows, cols] + jnp.dot(
                    xg[rows, aligned(last, local)], upw[aligned(last, local), cols], preferred_element_type=f32
                )

            hid[rows, cols] = wide[rows, cols].astype(bf16)
            for side, ready in ((1, part == (edge - 1) // part_rows), (0, part == parts - 1)):
                if ready:
                    halo_start(0, hid, hid_halo, side, cols, n)

    for i in (5, 6, 7):
        loads[i].wait()

    def waves_of(matrix, field, cols):
        return jnp.dot(matrix[...], field[:, cols], preferred_element_type=f32)

    def own_waves(waves, field, cols):
        waves[:, cols] = waves_of(fwd_own, field, cols)

    each(n_tiles, lambda n: own_waves(hid_waves, hid, aligned(n, tile)))

    half_waves = tap_waves.shape[0] // 2

    def product(left, other, cols, conjugate):
        lr, li = left[0:half_waves, cols], left[half_waves : 2 * half_waves, cols]
        rr, ri = other[0:half_waves, cols], other[half_waves : 2 * half_waves, cols]
        if conjugate:
            return jnp.concatenate([(lr * rr + li * ri).astype(bf16), (li * rr - lr * ri).astype(bf16)])
        return jnp.concatenate([(lr * rr - li * ri).astype(bf16), (li * rr + lr * ri).astype(bf16)])

    each(n_tiles, lambda n: halo_received(0, hid, hid_halo, aligned(n, tile), n))
    for n in range(n_tiles):
        cols = slice(n * tile, (n + 1) * tile)
        hid_waves[:, cols] = hid_waves[:, cols] + waves_of(fwd_halo, hid_halo, cols)
        preact = jnp.dot(inv[...], product(hid_waves, tap_waves, cols, True), preferred_element_type=f32)
        wide[:, cols] = preact
        act[:, cols] = (preact * jax.nn.sigmoid(preact)).astype(bf16)
        gather(0, cols, n).start()

    pl.when(at_end)(lambda: turn(1, xg, last))

    def project(left, weight, dest, out):
        @pl.loop(0, local // wtile)
        def _(n):
            rows = pl.ds(pl.multiple_of(dest * local + n * wtile, wtile), wtile)
            out[:, aligned(n, wtile)] = lax.dot_general(
                left[...], weight[rows, :], (((1,), (1,)), ((), ())), preferred_element_type=f32
            ).astype(out.dtype)

    def partial(i, dest, source, part):
        rows = slice(part * part_rows, (part + 1) * part_rows)
        return remote(
            sent.at[i, dest, rows], got.at[i, source, rows], sum_out_s.at[i, dest, part], sum_out_r.at[i, source, part],
            {"col": dest},
        )

    def passed(i, side, part):
        rows = slice(part * part_rows, (part + 1) * part_rows)
        return remote(
            sent.at[i, 0 if side else n_col - 1, rows], relay.at[i, side, rows],
            sum_out_s.at[i, 0 if side else n_col - 1, part], relay_r.at[i, side, part],
            {"col": n_col - 2 if side else 1},
        )

    def targets(m):
        far = n_col - 1 - m
        return (
            (0, far, far > col, jnp.logical_and(far == n_col - 1, col == 0), jnp.logical_and(far == n_col - 1, col == 1)),
            (1, m, m < col, jnp.logical_and(m == 0, last == 0), jnp.logical_and(m == 0, last == 1)),
        )

    def sums_begin(i, left, weight):
        @pl.loop(0, n_col - 1)
        def _(m):
            for side, dest, goes, ends, joins in targets(m):
                @pl.when(goes)
                def _():
                    project(left, weight, dest, sent.at[i, dest])
                    for part in range(parts):
                        pl.when(ends)(lambda: passed(i, side, part).start())
                        now = jnp.logical_not(jnp.logical_or(joins, at_end))
                        pl.when(now)(lambda: partial(i, dest, col, part).start())

    def sums_rest(i):
        @pl.when(at_end)
        def _():
            @pl.loop(0, n_col - 1)
            def _(m):
                for side, dest, goes, ends, _ in targets(m):
                    @pl.when(jnp.logical_and(goes, jnp.logical_not(ends)))
                    def _():
                        for part in range(parts):
                            partial(i, dest, col, part).start()

    def sums_join(i):
        for part in range(parts):
            rows = slice(part * part_rows, (part + 1) * part_rows)
            for side, dest, joins in ((0, n_col - 1, col == 1), (1, 0, last == 1)):
                @pl.when(joins)
                def _():
                    passed(i, side, part).wait_recv()
                    total = sent[i, dest, rows].astype(f32) + relay[i, side, rows].astype(f32)
                    sent[i, dest, rows] = total.astype(bf16)
                    partial(i, dest, col, part).start()

    def sums_end(i, residual, out):
        @pl.loop(0, n_col)
        def _(k):
            ends = jnp.logical_or(jnp.logical_and(k == 0, last == 0), jnp.logical_and(k == n_col - 1, col == 0))

            @pl.when(jnp.logical_and(k != col, jnp.logical_not(ends)))
            def _():
                for part in range(parts):
                    partial(i, col, k, part).wait_recv()
                own_sum[i] = own_sum[i] + got[i, k].astype(f32)

        out[...] = (residual[:, mine].astype(f32) + own_sum[i]).astype(bf16)

    def sums_sent(i):
        @pl.loop(0, n_col)
        def _(k):
            @pl.when(k != col)
            def _():
                for part in range(parts):
                    partial(i, k, col, part).wait_send()

    loads[4].wait()
    sums_begin(0, act, dnw)

    @pl.loop(0, n_col)
    def _(k):
        pl.when(k != col)(lambda: cot_copy(col, k).wait_recv())

    @pl.loop(0, n_tiles)
    def _(n):
        cols = aligned(n, tile)
        act_grad = jnp.dot(cg[...], dnw[:, cols], preferred_element_type=f32)
        preact = wide[:, cols]
        logistic = jax.nn.sigmoid(preact)
        grd[:, cols] = (act_grad * logistic * (1.0 + preact * (1.0 - logistic))).astype(bf16)
        halo_start(1, grd, grd_halo, 1, cols, n)
        halo_start(1, grd, grd_halo, 0, cols, n)

    sums_rest(0)
    each(n_col, lambda k: pl.when(k != col)(lambda: turn(0, cg, k)))
    each(n_tiles, lambda n: own_waves(grd_waves, grd, aligned(n, tile)))
    loads[9].wait()

    @pl.loop(0, n_tiles)
    def _(n):
        cols = aligned(n, tile)
        taps_out[:, cols] = jnp.dot(
            inv_taps[...], product(hid_waves, grd_waves, cols, True), preferred_element_type=f32
        ).astype(bf16)

    some, others = aligned(dp, channels // 2), aligned(1 - dp, channels // 2)
    whole_taps = remote(taps_out.at[:, others], taps_in, kg_s.at[0], kg_r.at[0], partner)
    whole_taps.start()
    project(act, dnw, col, own_sum.at[0])
    sums_join(0)

    each(n_tiles, lambda n: halo_received(1, grd, grd_halo, aligned(n, tile), n))
    for n in range(n_tiles):
        cols = slice(n * tile, (n + 1) * tile)
        grd_waves[:, cols] = grd_waves[:, cols] + waves_of(fwd_halo, grd_halo, cols)
        hgr[:, cols] = jnp.dot(
            inv[...], product(grd_waves, tap_waves, cols, False), preferred_element_type=f32
        ).astype(bf16)
        gather(1, cols, n).start()

    sums_begin(1, hgr, upw)

    def pair(i, j, cols, n):
        return remote(first_out.at[i, j, :, cols], first_in.at[i, j, :, cols], pair_s.at[i, j, n], pair_r.at[i, j, n], partner)

    def row_copy(i, to, source, cols, n):
        return remote(
            second_out.at[i, to, :, cols], second_in.at[i, source, :, cols], row_s.at[i, to, n], row_r.at[i, source, n],
            {"row": row_of(i, side_of(i, row), to)},
        )

    def outer(i, half, j, cols):
        index = half * n_row + row_of(i, side_of(i, row), j)
        return jnp.dot(
            turned[i, aligned(index, share)], right[i, :, cols], preferred_element_type=f32
        ) + jnp.dot(turned_in[i, half * n_half + j], right_in[i, :, cols], preferred_element_type=f32)

    def grad_for_partner(i, n):
        cols = aligned(n, tile)
        gather(i, cols, n).wait_recv()
        if i:
            rows_start(0, n)

        for j in range(n_half):
            first_out[i, j, :, cols] = outer(i, 1 - dp, j, cols).astype(bf16)
        for j in range(n_half):
            pair(i, j, cols, n).start()

    def grad_own(i, n):
        cols = aligned(n, tile)
        here = place_of(i, row)

        for j in range(n_half):
            pair(i, j, cols, n).wait_recv()
        for j in range(n_half):
            total = outer(i, dp, j, cols) + first_in[i, j, :, cols].astype(f32)
            second_out[i, j, :, cols] = total.astype(bf16)
        if i:
            rows_start(i, n)

    def rows_start(i, n):
        here = place_of(i, row)
        each(n_half, lambda j: pl.when(j != here)(lambda: row_copy(i, j, here, aligned(n, tile), n).start()))

    def grad_step(i, step):
        pl.when(step < n_tiles)(lambda: grad_for_partner(i, step))
        pl.when(jnp.logical_and(step > 0, step <= n_tiles))(lambda: grad_own(i, step - 1))

    def grad_finish(i, out):
        here = place_of(i, row)

        @pl.loop(0, n_tiles)
        def _(n):
            cols = aligned(n, tile)
            own_sum_tile = second_out[i, here, :, cols].astype(f32)
            for k in range(1, n_half):
                source = lax.rem(here + k, n_half)
                row_copy(i, here, source, cols, n).wait_recv()
                own_sum_tile = own_sum_tile + second_in[i, source, :, cols].astype(f32)
            out[:, cols] = own_sum_tile.astype(bf16)

    def pieces_received(i):
        @pl.loop(0, n_dp * n_half)
        def _(slot):
            index = (slot // n_half) * n_row + row_of(i, 1 - side_of(i, row), lax.rem(slot, n_half))
            pl.when(jnp.logical_or(i == 0, (index * share) // local != col))(lambda: piece(i, index).wait_recv())

    pieces_received(0)
    each(n_tiles + 1, lambda step: grad_step(0, step))
    sums_rest(1)
    whole_taps.wait_recv()
    share_out[...] = (taps_out[:, some].astype(f32) + taps_in[...].astype(f32)).astype(bf16)
    tap_share = share_out.shape[0] // n_row

    def taps_copy(k):
        peer = lax.rem(row + k, n_row)
        return remote(share_out.at[aligned(peer, tap_share)], share_in.at[k], kg_s.at[k], kg_r.at[k], {"row": peer})

    def taps_sum(k, source):
        target = half_out.at[aligned(source, tap_share)]
        return remote(
            half_out.at[aligned(row, tap_share)], target, sum_s.at[k], sum_r.at[k], {"row": lax.rem(row + k, n_row)}
        )

    each(n_row, lambda k: taps_copy(k).start(), 1)
    sums_end(0, xg, block_output)
    stores[0].start()
    sums_join(1)
    project(hgr, upw, col, own_sum.at[1])
    pieces_received(1)

    @pl.loop(0, n_tiles + 1)
    def _(step):
        grad_step(1, step)

    each(n_row, lambda k: taps_copy(k).wait_recv(), 1)
    my_taps = aligned(row, tap_share)
    total = share_out[my_taps].astype(f32)
    for k in range(1, n_row):
        total = total + share_in[k].astype(f32)
    half_out[my_taps] = total.astype(bf16)
    each(n_row, lambda k: taps_sum(k, row).start(), 1)
    sums_end(1, cg, input_grad)
    stores[1].start()
    each(n_row, lambda k: taps_sum(k, lax.rem(row + n_row - k, n_row)).wait_recv(), 1)
    halves = remote(half_out, half_in, kg_s.at[n_row], kg_r.at[n_row], partner)
    halves.start()
    n_taps = kernel.shape[0]
    kernel_grad[:, some] = half_out[...].astype(f32)[0:n_taps]
    grad_finish(1, up_grad)
    stores[2].start()
    halves.wait_recv()
    kernel_grad[:, others] = half_in[...].astype(f32)[0:n_taps]
    stores[4].start()
    grad_finish(0, down_grad)
    stores[3].start()

    for step in range(n_col - 1):
        for part in range(parts):
            for side in (1, -1):
                pl.when(hop_goes(side, step))(hop(side, step, part).wait_send)
    each(n_col, lambda k: pl.when(k != col)(lambda: cot_copy(k, col).wait_send()))
    for i in range(2):
        sums_sent(i)
        each(n_dp * n_row, lambda k: pl.when(leaves(i, k))(lambda: piece(i, k).wait_send()))

        @pl.loop(0, n_tiles)
        def _(n):
            cols = aligned(n, tile)
            halo_sent(i, (hid, grd)[i], (hid_halo, grd_halo)[i], cols, n)
            gather(i, cols, n).wait_send()
            here = place_of(i, row)
            for j in range(n_half):
                pair(i, j, cols, n).wait_send()
                pl.when(j != here)(lambda: row_copy(i, j, here, cols, n).wait_send())

    whole_taps.wait_send()
    each(n_row, lambda k: taps_copy(k).wait_send(), 1)
    each(n_row, lambda k: taps_sum(k, row).wait_send(), 1)
    halves.wait_send()
    for store in stores:
        store.wait()


def hand_on(*refs):
    arrived, done = refs[15], refs[16]
    fetches = [pltpu.make_async_copy(refs[i], refs[10 + i], arrived.at[i]) for i in range(5)]
    stores = [pltpu.make_async_copy(refs[10 + i], refs[5 + i], done.at[i]) for i in range(5)]
    for fetch in fetches:
        fetch.start()
    for fetch, store in zip(fetches, stores):
        fetch.wait()
        store.start()
    for store in stores:
        store.wait()


def on_device(inputs, up_weight, down_weight, kernel, cotangent):
    _, planes, tile_x, tile_y, local = inputs.shape
    n_dp, n_row, n_col = (lax.axis_size(name) for name in ("dp", "row", "col"))
    voxels = planes * tile_x * tile_y
    extended = voxels + 2 * HALO * tile_x * tile_y
    width, channels = up_weight.shape
    share = width // (n_dp * n_row)
    bf16, f32 = jnp.bfloat16, jnp.float32
    dma = pltpu.SemaphoreType.DMA
    taps = kernel.shape[0]
    tap_rows = -(-taps // (16 * n_row)) * 16 * n_row
    anywhere = pl.BlockSpec(memory_space=pl.ANY)
    matrices = transforms(planes, tile_x, tile_y, tap_rows)
    n_waves = matrices[0].shape[0]
    tile = min(256, channels)
    n_tiles = channels // tile
    edge = HALO * tile_x * tile_y
    n_half = n_row // 2
    parts = 2 if n_col <= 4 else 1
    out_types = (
        ((voxels, local), bf16), ((voxels, local), bf16), ((share, channels), bf16), ((share, channels), bf16),
        ((taps, channels), f32),
    )
    outs = pl.pallas_call(
        functools.partial(block_kernel, (planes, tile_x, tile_y, n_dp, n_row, n_col)),
        out_shape=tuple(jax.ShapeDtypeStruct(shape, dtype) for shape, dtype in out_types),
        in_specs=[anywhere] * 10,
        out_specs=(anywhere,) * 5,
        scratch_shapes=[
            *(pltpu.VMEM(shape, dtype) for shape, dtype in out_types),
            pltpu.VMEM(kernel.shape, f32),
            pltpu.VMEM((voxels, width), bf16),
            pltpu.VMEM((voxels, width), bf16),
            pltpu.VMEM((width, channels), bf16),
            pltpu.VMEM((width, channels), bf16),
            pltpu.VMEM((voxels, channels), bf16),
            pltpu.VMEM((voxels, channels), bf16),
            pltpu.VMEM((2 * edge, channels), bf16),
            pltpu.VMEM((2 * edge, channels), bf16),
            pltpu.VMEM((voxels, channels), f32),
            pltpu.VMEM((2, voxels, channels), bf16),
            pltpu.VMEM((2, voxels, channels), bf16),
            *(pltpu.VMEM(m.shape, bf16) for m in matrices),
            pltpu.VMEM((n_waves, channels), f32),
            pltpu.VMEM((n_waves, channels), f32),
            pltpu.VMEM((n_waves, channels), f32),
            pltpu.VMEM((2, n_col, voxels, local), bf16),
            pltpu.VMEM((2, n_col, voxels, local), bf16),
            pltpu.VMEM((2, 2, voxels, local), bf16),
            pltpu.VMEM((2, voxels, local), f32),
            pltpu.VMEM((2, width, voxels), bf16),
            pltpu.VMEM((2, n_dp * n_half, share, voxels), bf16),
            pltpu.VMEM((2, n_half, share, channels), bf16),
            pltpu.VMEM((2, n_half, share, channels), bf16),
            pltpu.VMEM((2, n_half, share, channels), bf16),
            pltpu.VMEM((2, n_half, share, channels), bf16),
            pltpu.VMEM((tap_rows, channels), bf16),
            pltpu.VMEM((tap_rows, channels // 2), bf16),
            pltpu.VMEM((tap_rows, channels // 2), bf16),
            pltpu.VMEM((n_row, tap_rows // n_row, channels // 2), bf16),
            pltpu.VMEM((tap_rows, channels // 2), bf16),
            pltpu.VMEM((tap_rows, channels // 2), bf16),
            dma((10,)), dma((5,)),
            dma((2, n_col, parts)), dma((2, n_col, parts)),
            dma((n_col,)), dma((n_col,)),
            dma((2, 2, n_tiles)), dma((2, 2, n_tiles)),
            dma((2, n_col, parts)), dma((2, n_col, parts)), dma((2, 2, parts)),
            dma((2, n_dp * n_half)), dma((2, n_dp * n_half)),
            dma((2, n_tiles)), dma((2, n_tiles)),
            dma((2, n_half, n_tiles)), dma((2, n_half, n_tiles)),
            dma((2, n_half, n_tiles)), dma((2, n_half, n_tiles)),
            dma((n_row + 1,)), dma((n_row + 1,)),
            dma((n_row,)), dma((n_row,)),
        ],
        compiler_params=pltpu.CompilerParams(
            collective_id=0, has_side_effects=True, vmem_limit_bytes=60 << 20
        ),
    )(inputs.reshape(voxels, local), cotangent.reshape(voxels, local), up_weight, down_weight, kernel,
      *map(jnp.asarray, matrices))
    outs = pl.pallas_call(
        hand_on,
        out_shape=tuple(jax.ShapeDtypeStruct(out.shape, out.dtype) for out in outs),
        in_specs=[anywhere] * 5,
        out_specs=(anywhere,) * 5,
        scratch_shapes=[pltpu.VMEM(out.shape, out.dtype) for out in outs] + [dma((5,)), dma((5,))],
    )(*outs)
    return (outs[0].reshape(inputs.shape), outs[1].reshape(inputs.shape)) + tuple(outs[2:])


def solution(mesh):
    placed = (
        P("dp", "row", None, None, "col"),
        P(None, "col"),
        P(None, "col"),
        P(None, "col"),
        P("dp", "row", None, None, "col"),
    )
    return jax.shard_map(
        on_device,
        mesh=mesh,
        in_specs=placed,
        out_specs=(
            P("dp", "row", None, None, "col"),
            P("dp", "row", None, None, "col"),
            P(("dp", "row"), "col"),
            P(("dp", "row"), "col"),
            P(None, "col"),
        ),
        check_vma=False,
    )
```
